32 devices in a mesh: dp: 4 (over x, core), ctx: 8 (over z, y).
Axes of the slice: x: 2, y: 2, z: 4, core: 2. Of those that a mesh axis runs over, the one named last changes fastest.
Arguments:
- queries: bfloat16 [16384, 32, 128], P(('dp', 'ctx')), may hold values from -8 to 8
- keys: bfloat16 [16384, 4, 128], P(('dp', 'ctx')), may hold values from -8 to 8
- values: bfloat16 [16384, 4, 128], P(('dp', 'ctx')), may hold values from -6 to 6
- doc_lengths: int32 [4, 8], P('dp'), may hold values from 1 to 1024, 4096 in all within a row
Outputs:
- attended: bfloat16 [16384, 32, 128], P(('dp', 'ctx'))
The draws below stay inside these ranges and needn't reach their ends.
All inputs are finite; a program needn't handle non-finite values.
Results may differ from the reference program's by a relative error of at most 0.0035.
Values may be sent and summed in bfloat16 or wider, within the bound.
A program may use at most 128 MiB of HBM per device.

```python
import math
import jax
import jax.numpy as jnp
import numpy as np
from jax import lax

QUERY_HEADS = 32
KEY_VALUE_HEADS = 4
HEAD_DIMENSION = 128
TILE_TOKENS = 512
SEQ = 4096
TOKEN_TOTAL = 16384
DOCS = 8
DOC_MOST = 1024
N_DP = 4
N_CTX = 8


def drawn_pair(key):
    queries = jnp.clip(jax.random.normal(jax.random.fold_in(key, 11), (TOKEN_TOTAL, QUERY_HEADS, HEAD_DIMENSION), jnp.float32), -4.0, 4.0)
    keys = jnp.clip(jax.random.normal(jax.random.fold_in(key, 12), (TOKEN_TOTAL, KEY_VALUE_HEADS, HEAD_DIMENSION), jnp.float32), -4.0, 4.0)
    return (queries, keys)


def draw_queries(key, part):
    return drawn_pair(key)[0].astype(jnp.bfloat16)


def draw_keys(key, part):
    return drawn_pair(key)[1].astype(jnp.bfloat16)


def level_of(own_key, extent, shards, least, top_value):
    gain, own = 1.0, jax.random.fold_in(own_key, 6)
    for axis_at, shards_of in shards:
        draws = jnp.exp(jax.random.uniform(jax.random.fold_in(own, axis_at), (shards_of,), jnp.float32, least / len(shards), top_value / len(shards)))
        gain = gain * jnp.repeat(draws, extent[axis_at] // shards_of).reshape([-1 if axis == axis_at else 1 for axis in range(len(extent))])
    return gain


def length_profile(count, total, most, lean):
    weights = [(1 << 20) // math.isqrt(rank ** lean) + 1 for rank in range(2, count + 1)]
    surplus, holding = total - most - (count - 1), [1] * (count - 1)
    while surplus > 0:
        free = [i for i in range(count - 1) if holding[i] < most]
        whole, remaining = sum([weights[i] for i in free]), surplus
        for i in free:
            more = min(most - holding[i], max(1, remaining * weights[i] // whole), surplus)
            holding[i] = holding[i] + more
            surplus = surplus - more
    return np.array([most] + holding)


def uneven_parts(key, amount, total, limit, slope):
    if amount == 2:
        one = jax.random.randint(key, (), max(1, total - limit), min(limit, total - 1) + 1)
        return jnp.stack([one, total - one])
    tallies = jnp.asarray(length_profile(amount, total, limit, slope), jnp.int32)
    pairs = (amount - 1) // 2
    giver, sink = tallies[1:1 + 2 * pairs:2], tallies[2:2 + 2 * pairs:2]
    room = jnp.minimum(giver - 1, limit - sink)
    moved = jax.random.randint(jax.random.fold_in(key, 1), (pairs,), 0, 1 << 20) % (room + 1)
    tallies = tallies.at[1:1 + 2 * pairs:2].set(giver - moved).at[2:2 + 2 * pairs:2].set(sink + moved)
    return tallies[jax.random.permutation(jax.random.fold_in(key, 2), amount)]


def centred(own_key, dims, scale, bound, shards=(), held_as=jnp.bfloat16):
    entries = jax.random.normal(own_key, dims, jnp.float32) * scale
    if len(shards) > 0:
        entries = level_of(own_key, dims, shards, -0.22, 0.18) * entries
    return jnp.clip(entries, min=-bound, max=bound).astype(held_as)


def setup_inputs(seed: int = 0) -> dict:
    seeds = jax.random.split(jax.random.key(seed), 5)
    queries = draw_queries(jax.random.fold_in(seeds[4], 71), 0)
    keys = draw_keys(jax.random.fold_in(seeds[4], 71), 0)
    values = centred(seeds[2], (TOKEN_TOTAL, KEY_VALUE_HEADS, HEAD_DIMENSION), 1.0, 6.0, ((0, 32),))
    doc_lengths = jax.vmap(lambda own: uneven_parts(own, DOCS, SEQ, DOC_MOST, 2))(jax.random.split(seeds[3], N_DP)).reshape((N_DP, DOCS)).astype(jnp.int32)
    return dict(queries=queries, keys=keys, values=values, doc_lengths=doc_lengths)


def doc_index(positions, lengths):
    doc_ends = jnp.cumsum(lengths)
    return lax.optimization_barrier(jnp.sum((positions[:, None] >= doc_ends[None, :]).astype(jnp.int32), axis=1))

def tile_partial(tile_queries, block_keys, block_values, query_pos, key_pos, lengths):
    tile_rows, head_count, head_width = tile_queries.shape
    kv_count = block_keys.shape[1]
    group_size = head_count // kv_count
    allowed = doc_index(query_pos, lengths)[:, None] == doc_index(key_pos, lengths)[None, :]
    allowed = allowed & (key_pos[None, :] <= query_pos[:, None]) & (key_pos[None, :] >= 0)
    score_scale = 1.0 / math.sqrt(head_width)
    grouped = tile_queries.reshape(tile_rows, kv_count, group_size, head_width).transpose(1, 0, 2, 3)
    key_heads = block_keys.transpose(1, 0, 2)
    value_heads = block_values.transpose(1, 0, 2)

    def one_head(operands):
        query_group, key_head, value_head = operands
        scores = jnp.einsum('tgd,ud->gtu', query_group.astype(jnp.float32), key_head.astype(jnp.float32)) * score_scale
        masked = jnp.where(allowed[None], scores, -1e+30)
        maxima = lax.optimization_barrier(jnp.max(masked, axis=-1))
        weights = jnp.where(allowed[None], jnp.exp(masked - maxima[..., None]), 0.0)
        sums = lax.optimization_barrier(jnp.sum(weights, axis=-1))
        rounded = weights.astype(jnp.bfloat16)
        outputs = jnp.einsum('gtu,ud->tgd', rounded.astype(jnp.float32), value_head.astype(jnp.float32))
        return (maxima, sums, outputs)
    maxima, sums, outputs = lax.map(one_head, (grouped, key_heads, value_heads))
    maxima = maxima.reshape(head_count, tile_rows)
    sums = sums.reshape(head_count, tile_rows)
    outputs = outputs.transpose(1, 0, 2, 3).reshape(tile_rows, head_count, head_width)
    return (maxima, sums, outputs)

def merge_tiles(partials):
    row_max = partials[0][0]
    for part_item in partials[1:]:
        row_max = jnp.maximum(row_max, part_item[0])
    denominator = 0.0
    weighted = 0.0
    for maxima, sums, outputs in partials:
        factor = jnp.exp(maxima - row_max)
        denominator = denominator + factor * sums
        weighted = weighted + factor.T[:, :, None] * outputs
    return (weighted / denominator.T[:, :, None]).astype(jnp.bfloat16)

def reference(queries, keys, values, doc_lengths):
    sequence_length = TILE_TOKENS * N_CTX
    key_padding = jnp.pad(keys.reshape(N_DP, sequence_length, KEY_VALUE_HEADS, HEAD_DIMENSION), ((0, 0), (2 * TILE_TOKENS, 0), (0, 0), (0, 0)))
    value_padding = jnp.pad(values.reshape(N_DP, sequence_length, KEY_VALUE_HEADS, HEAD_DIMENSION), ((0, 0), (2 * TILE_TOKENS, 0), (0, 0), (0, 0)))

    def one_tile(tile_index):
        batch_position = (tile_index // N_CTX).astype(jnp.int32)
        shard_index = (tile_index % N_CTX).astype(jnp.int32)
        tile_queries = lax.dynamic_slice_in_dim(queries, (tile_index * TILE_TOKENS).astype(jnp.int32), TILE_TOKENS, 0)
        lengths = lax.dynamic_index_in_dim(doc_lengths, batch_position, 0, False)
        query_pos = shard_index * TILE_TOKENS + jnp.arange(TILE_TOKENS, dtype=jnp.int32)
        partials = []
        for offset in (0, 1, 2):
            start_offset = ((shard_index + 2 - offset) * TILE_TOKENS).astype(jnp.int32)
            zero_value = jnp.zeros((), jnp.int32)
            block_keys = lax.dynamic_slice(key_padding, (batch_position, start_offset, zero_value, zero_value), (1, TILE_TOKENS, KEY_VALUE_HEADS, HEAD_DIMENSION))[0]
            block_values = lax.dynamic_slice(value_padding, (batch_position, start_offset, zero_value, zero_value), (1, TILE_TOKENS, KEY_VALUE_HEADS, HEAD_DIMENSION))[0]
            partials.append(tile_partial(tile_queries, block_keys, block_values, query_pos, query_pos - offset * TILE_TOKENS, lengths))
        return merge_tiles(partials)
    attended = lax.map(one_tile, jnp.arange(N_DP * N_CTX, dtype=jnp.int32))
    return attended.reshape(TOKEN_TOTAL, QUERY_HEADS, HEAD_DIMENSION)
```

```python
import functools
import math

import jax
import jax.numpy as jnp
from jax import lax
from jax.experimental import pallas as pl
from jax.experimental.pallas import tpu as pltpu
from jax.sharding import PartitionSpec as P

LANES = 128
BLOCK = 64
PIECES = 2
MASKED = -1e30
MESH = pl.DeviceIdType.MESH


def kernel(count, lengths, q_hbm, k_hbm, v_hbm, out, own, win, qbuf, raw, flat, hot, bias_own,
           bias_win, scores_a, scores_b, tops_a, tops_b, state, state_top, qsem, rawsem,
           far_send, far_recv, near_send, near_recv):
    rows, heads, width = k_hbm.shape
    group = q_hbm.shape[1] // heads
    blocks = rows // BLOCK
    half = blocks // 2
    piece_rows = rows // PIECES
    per_head = 2 * PIECES
    chunks = per_head * heads
    ahead = per_head
    me = lax.axis_index("ctx")
    odd = lax.rem(me, 2) == 1
    even = jnp.logical_not(odd)
    partner = jnp.where(odd, me - 1, me + 1)
    has_up = me + 2 < count
    has_down = me >= 2

    barrier = pltpu.get_barrier_semaphore()

    def greet(other):
        pl.semaphore_signal(barrier, inc=1, device_id={"ctx": other}, device_id_type=MESH)

    def q_copy(h):
        return pltpu.make_async_copy(
            q_hbm.at[:, pl.ds(h * group, group), :], qbuf.at[h], qsem.at[h]
        )

    def raw_copy(part):
        return pltpu.make_async_copy((k_hbm, v_hbm)[part], raw.at[part], rawsem.at[part])

    def place(c):
        h, rest = lax.div(c, per_head), lax.rem(c, per_head)
        part, piece = lax.div(rest, PIECES), lax.rem(rest, PIECES)
        return part, h, pl.multiple_of(piece * piece_rows, piece_rows)

    def far_copy(c):
        part, h, first = place(c)
        return pltpu.make_async_remote_copy(
            src_ref=own.at[part, h, pl.ds(first, piece_rows), :],
            dst_ref=win.at[part, h, pl.ds(first, piece_rows), :],
            send_sem=far_send.at[c],
            recv_sem=far_recv.at[c],
            device_id={"ctx": me + 2},
            device_id_type=MESH,
        )

    def near_copy(c):
        part, h, first = place(c)
        return pltpu.make_async_remote_copy(
            src_ref=own.at[part, h, pl.ds(first, piece_rows), :],
            dst_ref=win.at[part, h, pl.ds(rows + first, piece_rows), :],
            send_sem=near_send.at[c],
            recv_sem=near_recv.at[c],
            device_id={"ctx": partner},
            device_id_type=MESH,
        )

    def relay_copy(c):
        part, h, first = place(c)
        return pltpu.make_async_remote_copy(
            src_ref=win.at[part, h, pl.ds(first, piece_rows), :],
            dst_ref=win.at[part, h, pl.ds(rows + first, piece_rows), :],
            send_sem=near_send.at[c],
            recv_sem=near_recv.at[c],
            device_id={"ctx": partner},
            device_id_type=MESH,
        )

    def launch(c):
        @pl.when(has_up)
        def _():
            far_copy(c).start()

        @pl.when(even)
        def _():
            near_copy(c).start()

    def settle(c):
        @pl.when(has_up)
        def _():
            far_copy(c).wait_send()

        @pl.when(even)
        def _():
            near_copy(c).wait_send()

    def pump(c):
        settle(c)

        @pl.when(c + ahead < chunks)
        def _():
            launch(c + ahead)

        @pl.when(odd & has_down)
        def _():
            far_copy(c).wait_recv()
            relay_copy(c).start()

    def arrive(h, part):
        for piece in range(PIECES):
            c = h * per_head + part * PIECES + piece

            @pl.when(even & has_down)
            def _():
                far_copy(c).wait_recv()

            @pl.when(me >= 1)
            def _():
                near_copy(c).wait_recv()

    greet(partner)

    @pl.when(has_up)
    def _():
        greet(me + 2)

    @pl.when(has_down)
    def _():
        greet(me - 2)

    for part in range(2):
        raw_copy(part).start()
    for h in range(heads):
        q_copy(h).start()

    for part in range(2):
        raw_copy(part).wait()
        flat[...] = raw[part].astype(jnp.float32).reshape(rows * heads, width)
        for h in range(heads):
            own[part, h] = flat[pl.ds(h, rows, stride=heads), :].astype(own.dtype)
        if part == 0:
            pl.semaphore_wait(
                barrier, 1 + has_up.astype(jnp.int32) + has_down.astype(jnp.int32)
            )
        for piece in range(PIECES):
            launch(part * PIECES + piece)

    @pl.when(me < 2)
    def _():
        win[:, :, 0:rows, :] = jnp.zeros((2, heads, rows, width), win.dtype)

    @pl.when(me < 1)
    def _():
        win[:, :, rows : 2 * rows, :] = jnp.zeros((2, heads, rows, width), win.dtype)

    row_token = lax.broadcasted_iota(jnp.int32, (BLOCK, group, LANES), 0)
    lane = lax.broadcasted_iota(jnp.int32, (BLOCK, group, LANES), 2)
    hot[...] = (
        jnp.where(row_token == lane, 1.0, 0.0).reshape(BLOCK * group, LANES).astype(hot.dtype)
    )

    def fill_bias(block, carry):
        base = me * rows
        token = base + block * BLOCK + lax.broadcasted_iota(jnp.int32, (1, LANES), 1)
        first = jnp.zeros((1, LANES), jnp.int32)
        end = jnp.int32(0)
        for d in range(lengths.shape[1]):
            end = end + lengths[0, d]
            first = jnp.where(token >= end, end, first)
        key = base + lax.broadcasted_iota(jnp.int32, (rows, LANES), 0)
        allowed = (key >= first) & (key <= token)
        bias_own[block] = jnp.where(allowed, 0.0, MASKED).astype(bias_own.dtype)
        key = base - 2 * rows + lax.broadcasted_iota(jnp.int32, (2 * rows, LANES), 0)
        bias_win[block] = jnp.where(key >= first, 0.0, MASKED).astype(bias_win.dtype)
        return carry

    lax.fori_loop(0, blocks, fill_bias, 0)

    factor = math.log2(math.e) / math.sqrt(width)

    def queries_of(h, block):
        at = pl.ds(pl.multiple_of(block * BLOCK, BLOCK), BLOCK)
        q = qbuf[h, at].reshape(BLOCK * group, width)
        return jnp.concatenate([q, hot[...]], axis=1)

    def product(q, keys):
        return lax.dot_general(
            q, keys, (((1,), (1,)), ((), ())), preferred_element_type=jnp.float32
        )

    def weigh(scores, tops, values):
        span = values.shape[0]
        ones = jnp.ones((span, LANES), values.dtype)
        top = jnp.concatenate([tops[...]] * (span // LANES), axis=1)
        weights = jnp.exp2((scores[:, 0:span] - top) * factor).astype(values.dtype)
        return jnp.dot(
            weights, jnp.concatenate([values, ones], axis=1), preferred_element_type=jnp.float32
        )

    def score_own(h, block, span, scores, tops):
        keys = jnp.concatenate([own[0, h, 0:span, :], bias_own[block, 0:span]], axis=1)
        found = product(queries_of(h, block), keys)
        scores[:, 0:span] = found
        tops[...] = jnp.broadcast_to(jnp.max(found, axis=1, keepdims=True), tops.shape)

    def value_own(h, block, span, scores, tops):
        at = h * blocks + block
        state[at] = weigh(scores, tops, own[1, h, 0:span, :])
        state_top[at] = tops[...]

    def score_win(h, block, start, scores, tops):
        span = 2 * rows - start
        keys = jnp.concatenate([win[0, h, start:, :], bias_win[block, start:]], axis=1)
        found = product(queries_of(h, block), keys)
        scores[:, 0:span] = found
        best = jnp.broadcast_to(jnp.max(found, axis=1, keepdims=True), tops.shape)
        tops[...] = jnp.maximum(best, state_top[h * blocks + block])

    def value_win(h, block, start, scores, tops):
        at = h * blocks + block
        total = weigh(scores, tops, win[1, h, start:, :])
        scale = jnp.exp2((state_top[at] - tops[...]) * factor)
        total = total + state[at] * jnp.concatenate([scale, scale], axis=1)
        result = total[:, :width] / total[:, width : 2 * width]
        out[
            pl.ds(pl.multiple_of(block * BLOCK, BLOCK), BLOCK),
            pl.ds(pl.multiple_of(h * group, group), group),
            :,
        ] = result.reshape(BLOCK, group, width).astype(out.dtype)

    laps = heads * half
    first_pump = laps - per_head - 3
    near_half, far_half = rows // 2, 0

    for h in range(heads):
        q_copy(h).wait()

    score_own(0, 0, rows // 2, scores_a, tops_a)

    def own_lap(lap, carry):
        h, j = lax.div(lap, half), lax.rem(lap, half)
        later = jnp.minimum(lap + 1, laps - 1)

        @pl.when((lap >= first_pump) & (lap < first_pump + per_head))
        def _():
            pump(lap - first_pump)

        score_own(h, j + half, rows, scores_b, tops_b)
        value_own(h, j, rows // 2, scores_a, tops_a)
        score_own(lax.div(later, half), lax.rem(later, half), rows // 2, scores_a, tops_a)
        value_own(h, j + half, rows, scores_b, tops_b)
        return carry

    lax.fori_loop(0, laps, own_lap, 0)

    arrive(0, 0)
    score_win(0, 0, far_half, scores_a, tops_a)

    def win_lap(lap, carry):
        h, j = lax.div(lap, half), lax.rem(lap, half)
        later = jnp.minimum(lap + 1, laps - 1)

        @pl.when(j == 0)
        def _():
            arrive(h, 1)

        @pl.when(h + 1 < heads)
        def _():
            pump((h + 1) * per_head + j)

        @pl.when((j == half - 1) & (h + 1 < heads))
        def _():
            arrive(h + 1, 0)

        score_win(h, j + half, near_half, scores_b, tops_b)
        value_win(h, j, far_half, scores_a, tops_a)
        score_win(lax.div(later, half), lax.rem(later, half), far_half, scores_a, tops_a)
        value_win(h, j + half, near_half, scores_b, tops_b)
        return carry

    lax.fori_loop(0, laps, win_lap, 0)

    @pl.when(odd & has_down)
    def _():
        for c in range(chunks):
            relay_copy(c).wait_send()


def body(count, queries, keys, values, doc_lengths):
    rows, query_heads, width = queries.shape
    heads = keys.shape[1]
    group = query_heads // heads
    blocks = rows // BLOCK
    chunks = 2 * PIECES * heads
    any_space = pl.BlockSpec(memory_space=pl.ANY)
    return pl.pallas_call(
        functools.partial(kernel, count),
        out_shape=pltpu.VMEM(queries.shape, queries.dtype),
        in_specs=[pl.BlockSpec(memory_space=pltpu.SMEM), any_space, any_space, any_space],
        out_specs=pl.BlockSpec(memory_space=pltpu.VMEM),
        scratch_shapes=[
            pltpu.VMEM((2, heads, rows, width), keys.dtype),
            pltpu.VMEM((2, heads, 2 * rows, width), keys.dtype),
            pltpu.VMEM((heads, rows, group, width), queries.dtype),
            pltpu.VMEM((2, rows, heads, width), keys.dtype),
            pltpu.VMEM((rows * heads, width), jnp.float32),
            pltpu.VMEM((BLOCK * group, LANES), queries.dtype),
            pltpu.VMEM((blocks, rows, LANES), queries.dtype),
            pltpu.VMEM((blocks, 2 * rows, LANES), queries.dtype),
            pltpu.VMEM((BLOCK * group, 2 * rows), jnp.float32),
            pltpu.VMEM((BLOCK * group, 3 * rows // 2), jnp.float32),
            pltpu.VMEM((BLOCK * group, LANES), jnp.float32),
            pltpu.VMEM((BLOCK * group, LANES), jnp.float32),
            pltpu.VMEM((heads * blocks, BLOCK * group, 2 * width), jnp.float32),
            pltpu.VMEM((heads * blocks, BLOCK * group, LANES), jnp.float32),
            pltpu.SemaphoreType.DMA((heads,)),
            pltpu.SemaphoreType.DMA((2,)),
            pltpu.SemaphoreType.DMA((chunks,)),
            pltpu.SemaphoreType.DMA((chunks,)),
            pltpu.SemaphoreType.DMA((chunks,)),
            pltpu.SemaphoreType.DMA((chunks,)),
        ],
        compiler_params=pltpu.CompilerParams(
            collective_id=0, has_side_effects=True, vmem_limit_bytes=52 * 1024 * 1024
        ),
    )(doc_lengths, queries, keys, values)


def solution(mesh):
    placed = (
        P(("dp", "ctx"), None, None),
        P(("dp", "ctx"), None, None),
        P(("dp", "ctx"), None, None),
        P("dp", None),
    )
    return jax.shard_map(
        functools.partial(body, mesh.shape["ctx"]),
        mesh=mesh,
        in_specs=placed,
        out_specs=P(("dp", "ctx"), None, None),
        check_vma=False,
    )
```

```python
import functools
import math

import jax
import jax.numpy as jnp
from jax import lax
from jax.experimental import pallas as pl
from jax.experimental.pallas import tpu as pltpu
from jax.sharding import PartitionSpec as P

LANES = 128
BLOCK = 64
PIECES = 2
STRIDE = 2
MASKED = -1e30
MESH = pl.DeviceIdType.MESH


def kernel(count, lengths, q_hbm, k_hbm, v_hbm, out, own, win, qbuf, raw, flat, hot, bias_own,
           bias_win, scores_a, scores_b, tops_a, tops_b, state, state_top, qsem, rawsem,
           far_send, far_recv, near_send, near_recv):
    rows, heads, width = k_hbm.shape
    group = q_hbm.shape[1] // heads
    blocks = rows // BLOCK
    half = blocks // 2
    piece_rows = rows // PIECES
    per_head = 2 * PIECES
    chunks = per_head * heads
    me = lax.axis_index("ctx")
    odd = lax.rem(me, 2) == 1
    even = jnp.logical_not(odd)
    partner = jnp.where(odd, me - 1, me + 1)
    has_up = me + 2 < count
    has_down = me >= 2

    barrier = pltpu.get_barrier_semaphore()

    def greet(other):
        pl.semaphore_signal(barrier, inc=1, device_id={"ctx": other}, device_id_type=MESH)

    def q_copy(h):
        return pltpu.make_async_copy(
            q_hbm.at[:, pl.ds(h * group, group), :], qbuf.at[h], qsem.at[h]
        )

    def raw_copy(part):
        return pltpu.make_async_copy((k_hbm, v_hbm)[part], raw.at[part], rawsem.at[part])

    def place(c):
        h, rest = lax.div(c, per_head), lax.rem(c, per_head)
        part, piece = lax.div(rest, PIECES), lax.rem(rest, PIECES)
        return part, h, pl.multiple_of(piece * piece_rows, piece_rows)

    def far_copy(c):
        part, h, first = place(c)
        return pltpu.make_async_remote_copy(
            src_ref=own.at[part, h, pl.ds(first, piece_rows), :],
            dst_ref=win.at[part, h, pl.ds(first, piece_rows), :],
            send_sem=far_send.at[c],
            recv_sem=far_recv.at[c],
            device_id={"ctx": me + 2},
            device_id_type=MESH,
        )

    def near_copy(c):
        part, h, first = place(c)
        return pltpu.make_async_remote_copy(
            src_ref=own.at[part, h, pl.ds(first, piece_rows), :],
            dst_ref=win.at[part, h, pl.ds(rows + first, piece_rows), :],
            send_sem=near_send.at[c],
            recv_sem=near_recv.at[c],
            device_id={"ctx": partner},
            device_id_type=MESH,
        )

    def relay_copy(c):
        part, h, first = place(c)
        return pltpu.make_async_remote_copy(
            src_ref=win.at[part, h, pl.ds(first, piece_rows), :],
            dst_ref=win.at[part, h, pl.ds(rows + first, piece_rows), :],
            send_sem=near_send.at[c],
            recv_sem=near_recv.at[c],
            device_id={"ctx": partner},
            device_id_type=MESH,
        )

    def launch(c):
        @pl.when(has_up)
        def _():
            far_copy(c).start()

        @pl.when(even)
        def _():
            near_copy(c).start()

    def forward(c):
        @pl.when(odd & has_down)
        def _():
            far_copy(c).wait_recv()
            relay_copy(c).start()

    def forward_two(c, least):
        for piece in range(2):

            @pl.when((c + piece >= least) & (c + piece < chunks))
            def _():
                forward(c + piece)

    def arrive(h, part):
        for piece in range(PIECES):
            c = h * per_head + part * PIECES + piece

            @pl.when(even & has_down)
            def _():
                far_copy(c).wait_recv()

            @pl.when(me >= 1)
            def _():
                near_copy(c).wait_recv()

    greet(partner)

    @pl.when(has_up)
    def _():
        greet(me + 2)

    @pl.when(has_down)
    def _():
        greet(me - 2)

    for part in range(2):
        raw_copy(part).start()
    for part in range(2):
        raw_copy(part).wait()
        flat[...] = raw[part].astype(jnp.float32).reshape(rows * heads, width)
        for h in range(heads):
            own[part, h] = flat[pl.ds(h, rows, stride=heads), :].astype(own.dtype)
        if part == 0:
            pl.semaphore_wait(
                barrier, 1 + has_up.astype(jnp.int32) + has_down.astype(jnp.int32)
            )
            for c in range(PIECES):
                launch(c)

    def launch_rest(c, carry):
        launch(c)
        return carry

    lax.fori_loop(PIECES, chunks, launch_rest, 0)

    for h in range(heads):
        q_copy(h).start()

    @pl.when(me < 2)
    def _():
        win[:, :, 0:rows, :] = jnp.zeros((2, heads, rows, width), win.dtype)

    @pl.when(me < 1)
    def _():
        win[:, :, rows : 2 * rows, :] = jnp.zeros((2, heads, rows, width), win.dtype)

    row_token = lax.broadcasted_iota(jnp.int32, (BLOCK, group, LANES), 0)
    lane = lax.broadcasted_iota(jnp.int32, (BLOCK, group, LANES), 2)
    hot[...] = (
        jnp.where(row_token == lane, 1.0, 0.0).reshape(BLOCK * group, LANES).astype(hot.dtype)
    )

    def fill_bias(block, carry):
        base = me * rows
        token = base + block * BLOCK + lax.broadcasted_iota(jnp.int32, (1, LANES), 1)
        first = jnp.zeros((1, LANES), jnp.int32)
        end = jnp.int32(0)
        for d in range(lengths.shape[1]):
            end = end + lengths[0, d]
            first = jnp.where(token >= end, end, first)
        key = base + lax.broadcasted_iota(jnp.int32, (rows, LANES), 0)
        allowed = (key >= first) & (key <= token)
        bias_own[block] = jnp.where(allowed, 0.0, MASKED).astype(bias_own.dtype)
        key = base - 2 * rows + lax.broadcasted_iota(jnp.int32, (2 * rows, LANES), 0)
        bias_win[block] = jnp.where(key >= first, 0.0, MASKED).astype(bias_win.dtype)
        return carry

    lax.fori_loop(0, blocks, fill_bias, 0)

    factor = math.log2(math.e) / math.sqrt(width)

    def queries_of(h, block):
        at = pl.ds(pl.multiple_of(block * BLOCK, BLOCK), BLOCK)
        q = qbuf[h, at].reshape(BLOCK * group, width)
        return jnp.concatenate([q, hot[...]], axis=1)

    def product(q, keys):
        return lax.dot_general(
            q, keys, (((1,), (1,)), ((), ())), preferred_element_type=jnp.float32
        )

    def weigh(scores, tops, values):
        span = values.shape[0]
        ones = jnp.ones((span, LANES), values.dtype)
        top = jnp.concatenate([tops[...]] * (span // LANES), axis=1)
        weights = jnp.exp2((scores[:, 0:span] - top) * factor).astype(values.dtype)
        return jnp.dot(
            weights, jnp.concatenate([values, ones], axis=1), preferred_element_type=jnp.float32
        )

    def score_own(h, block, span, scores, tops):
        keys = jnp.concatenate([own[0, h, 0:span, :], bias_own[block, 0:span]], axis=1)
        found = product(queries_of(h, block), keys)
        scores[:, 0:span] = found
        tops[...] = jnp.broadcast_to(jnp.max(found, axis=1, keepdims=True), tops.shape)

    def value_own(h, block, span, scores, tops):
        at = h * blocks + block
        state[at] = weigh(scores, tops, own[1, h, 0:span, :])
        state_top[at] = tops[...]

    def score_win(h, block, start, scores, tops):
        span = 2 * rows - start
        keys = jnp.concatenate([win[0, h, start:, :], bias_win[block, start:]], axis=1)
        found = product(queries_of(h, block), keys)
        scores[:, 0:span] = found
        best = jnp.broadcast_to(jnp.max(found, axis=1, keepdims=True), tops.shape)
        tops[...] = jnp.maximum(best, state_top[h * blocks + block])

    def value_win(h, block, start, scores, tops):
        at = h * blocks + block
        total = weigh(scores, tops, win[1, h, start:, :])
        scale = jnp.exp2((state_top[at] - tops[...]) * factor)
        total = total + state[at] * jnp.concatenate([scale, scale], axis=1)
        result = total[:, :width] / total[:, width : 2 * width]
        out[
            pl.ds(pl.multiple_of(block * BLOCK, BLOCK), BLOCK),
            pl.ds(pl.multiple_of(h * group, group), group),
            :,
        ] = result.reshape(BLOCK, group, width).astype(out.dtype)

    pairs = heads * half
    near_half, far_half = rows // 2, 0

    def pair_at(index):
        index = jnp.minimum(index, pairs - 1)
        return lax.div(index, half), lax.rem(index, half)

    for h in range(heads):
        q_copy(h).wait()

    score_own(0, 0, rows // 2, scores_a, tops_a)

    def own_lap(lap, carry):
        forward(lax.div(3 * lap, 2))

        @pl.when(lax.rem(lap, 2) == 1)
        def _():
            forward(lax.div(3 * lap, 2) + 1)

        for i in range(half):
            h, j = pair_at(lap * half + i)
            next_h, next_j = pair_at(lap * half + i + 1)
            score_own(h, j + half, rows, scores_b, tops_b)
            value_own(h, j, rows // 2, scores_a, tops_a)
            score_own(next_h, next_j, rows // 2, scores_a, tops_a)
            value_own(h, j + half, rows, scores_b, tops_b)
        return carry

    lax.fori_loop(0, heads, own_lap, 0)

    arrive(0, 0)
    score_win(0, 0, far_half, scores_a, tops_a)
    laps = half // STRIDE
    early = 3 * heads // 2

    def win_lap(lap, carry):
        h, part = lax.div(lap, laps), lax.rem(lap, laps)

        forward_two(2 * lap + early - 1, early)

        @pl.when(part == 0)
        def _():
            arrive(h, 1)

        @pl.when((part == laps - 1) & (h + 1 < heads))
        def _():
            arrive(h + 1, 0)

        for i in range(STRIDE):
            h, j = pair_at(lap * STRIDE + i)
            next_h, next_j = pair_at(lap * STRIDE + i + 1)
            score_win(h, j + half, near_half, scores_b, tops_b)
            value_win(h, j, far_half, scores_a, tops_a)
            score_win(next_h, next_j, far_half, scores_a, tops_a)
            value_win(h, j + half, near_half, scores_b, tops_b)
        return carry

    lax.fori_loop(0, heads * laps, win_lap, 0)

    for c in range(chunks):

        @pl.when(has_up)
        def _():
            far_copy(c).wait_send()

        @pl.when(even | has_down)
        def _():
            near_copy(c).wait_send()


def body(count, queries, keys, values, doc_lengths):
    rows, query_heads, width = queries.shape
    heads = keys.shape[1]
    group = query_heads // heads
    blocks = rows // BLOCK
    chunks = 2 * PIECES * heads
    any_space = pl.BlockSpec(memory_space=pl.ANY)
    return pl.pallas_call(
        functools.partial(kernel, count),
        out_shape=pltpu.VMEM(queries.shape, queries.dtype),
        in_specs=[pl.BlockSpec(memory_space=pltpu.SMEM), any_space, any_space, any_space],
        out_specs=pl.BlockSpec(memory_space=pltpu.VMEM),
        scratch_shapes=[
            pltpu.VMEM((2, heads, rows, width), keys.dtype),
            pltpu.VMEM((2, heads, 2 * rows, width), keys.dtype),
            pltpu.VMEM((heads, rows, group, width), queries.dtype),
            pltpu.VMEM((2, rows, heads, width), keys.dtype),
            pltpu.VMEM((rows * heads, width), jnp.float32),
            pltpu.VMEM((BLOCK * group, LANES), queries.dtype),
            pltpu.VMEM((blocks, rows, LANES), queries.dtype),
            pltpu.VMEM((blocks, 2 * rows, LANES), queries.dtype),
            pltpu.VMEM((BLOCK * group, 2 * rows), jnp.float32),
            pltpu.VMEM((BLOCK * group, 3 * rows // 2), jnp.float32),
            pltpu.VMEM((BLOCK * group, LANES), jnp.float32),
            pltpu.VMEM((BLOCK * group, LANES), jnp.float32),
            pltpu.VMEM((heads * blocks, BLOCK * group, 2 * width), jnp.float32),
            pltpu.VMEM((heads * blocks, BLOCK * group, LANES), jnp.float32),
            pltpu.SemaphoreType.DMA((heads,)),
            pltpu.SemaphoreType.DMA((2,)),
            pltpu.SemaphoreType.DMA((chunks,)),
            pltpu.SemaphoreType.DMA((chunks,)),
            pltpu.SemaphoreType.DMA((chunks,)),
            pltpu.SemaphoreType.DMA((chunks,)),
        ],
        compiler_params=pltpu.CompilerParams(
            collective_id=0, has_side_effects=True, vmem_limit_bytes=52 * 1024 * 1024
        ),
    )(doc_lengths, queries, keys, values)


def solution(mesh):
    placed = (
        P(("dp", "ctx"), None, None),
        P(("dp", "ctx"), None, None),
        P(("dp", "ctx"), None, None),
        P("dp", None),
    )
    return jax.shard_map(
        functools.partial(body, mesh.shape["ctx"]),
        mesh=mesh,
        in_specs=placed,
        out_specs=P(("dp", "ctx"), None, None),
        check_vma=False,
    )
```

```python
import functools
import math

import jax
import jax.numpy as jnp
from jax import lax
from jax.experimental import pallas as pl
from jax.experimental.pallas import tpu as pltpu
from jax.sharding import PartitionSpec as P

LANES = 128
BLOCK = 64
PIECES = 2
STRIDE = 2
MASKED = -1e30
MESH = pl.DeviceIdType.MESH


def product(q, keys):
    return lax.dot_general(q, keys, (((1,), (1,)), ((), ())), preferred_element_type=jnp.float32)


def rate_of(width):
    return math.log2(math.e) / math.sqrt(width)


def weigh(scores, tops, values):
    span, width = values.shape
    ones = jnp.ones((span, LANES), values.dtype)
    top = jnp.concatenate([tops[...]] * (span // LANES), axis=1)
    weights = jnp.exp2((scores[:, 0:span] - top) * rate_of(width)).astype(values.dtype)
    return jnp.dot(
        weights, jnp.concatenate([values, ones], axis=1), preferred_element_type=jnp.float32
    )


def score_tile(q, keys, bias, before, scores, tops):
    found = product(q, jnp.concatenate([keys, bias], axis=1))
    scores[:, 0 : keys.shape[0]] = found
    best = jnp.broadcast_to(jnp.max(found, axis=1, keepdims=True), tops.shape)
    tops[...] = best if before is None else jnp.maximum(best, before)


def normalized(total):
    width = total.shape[1] // 2
    return total[:, :width] / total[:, width:]


def merged(total, state, state_top, tops):
    scale = jnp.exp2((state_top - tops) * rate_of(total.shape[1] // 2))
    return normalized(total + state * jnp.concatenate([scale, scale], axis=1))


def gather_kernel(count, lengths, q_hbm, k_hbm, v_hbm, out, last_win, last_q, hot, bias_win,
                  last_state, last_top, own, win, qbuf, state, state_top, raw, flat, bias_own,
                  scores_a, scores_b, tops_a, tops_b, qsem, rawsem, far_send, far_recv, near_send, near_recv):
    rows, heads, width = k_hbm.shape
    group = q_hbm.shape[1] // heads
    blocks = rows // BLOCK
    half = blocks // 2
    piece_rows = rows // PIECES
    per_head = 2 * PIECES
    chunks = per_head * heads
    me = lax.axis_index("ctx")
    odd = lax.rem(me, 2) == 1
    even = jnp.logical_not(odd)
    partner = jnp.where(odd, me - 1, me + 1)
    has_up = me + 2 < count
    has_down = me >= 2

    barrier = pltpu.get_barrier_semaphore()

    def greet(other):
        pl.semaphore_signal(barrier, inc=1, device_id={"ctx": other}, device_id_type=MESH)

    def q_copy(h):
        return pltpu.make_async_copy(
            q_hbm.at[:, pl.ds(h * group, group), :], qbuf.at[h], qsem.at[h]
        )

    def raw_copy(part):
        return pltpu.make_async_copy((k_hbm, v_hbm)[part], raw.at[part], rawsem.at[part])

    def place(c):
        h, rest = lax.div(c, per_head), lax.rem(c, per_head)
        part, piece = lax.div(rest, PIECES), lax.rem(rest, PIECES)
        return part, h, pl.multiple_of(piece * piece_rows, piece_rows)

    def far_copy(c):
        part, h, first = place(c)
        return pltpu.make_async_remote_copy(
            src_ref=own.at[part, h, pl.ds(first, piece_rows), :],
            dst_ref=win.at[part, h, pl.ds(first, piece_rows), :],
            send_sem=far_send.at[c],
            recv_sem=far_recv.at[c],
            device_id={"ctx": me + 2},
            device_id_type=MESH,
        )

    def near_copy(c):
        part, h, first = place(c)
        return pltpu.make_async_remote_copy(
            src_ref=own.at[part, h, pl.ds(first, piece_rows), :],
            dst_ref=win.at[part, h, pl.ds(rows + first, piece_rows), :],
            send_sem=near_send.at[c],
            recv_sem=near_recv.at[c],
            device_id={"ctx": partner},
            device_id_type=MESH,
        )

    def relay_copy(c):
        part, h, first = place(c)
        return pltpu.make_async_remote_copy(
            src_ref=win.at[part, h, pl.ds(first, piece_rows), :],
            dst_ref=win.at[part, h, pl.ds(rows + first, piece_rows), :],
            send_sem=near_send.at[c],
            recv_sem=near_recv.at[c],
            device_id={"ctx": partner},
            device_id_type=MESH,
        )

    def launch(c):
        @pl.when(has_up)
        def _():
            far_copy(c).start()

        @pl.when(even)
        def _():
            near_copy(c).start()

    def forward(c):
        @pl.when(odd & has_down)
        def _():
            far_copy(c).wait_recv()
            relay_copy(c).start()

    def forward_some(first, limit):
        for c in (first, first + 1):

            @pl.when(c < limit)
            def _():
                forward(c)

    def arrive(h, part):
        for piece in range(PIECES):
            c = h * per_head + part * PIECES + piece

            @pl.when(even & has_down)
            def _():
                far_copy(c).wait_recv()

            @pl.when(me >= 1)
            def _():
                near_copy(c).wait_recv()

    greet(partner)

    @pl.when(has_up)
    def _():
        greet(me + 2)

    @pl.when(has_down)
    def _():
        greet(me - 2)

    for part in range(2):
        raw_copy(part).start()
    for part in range(2):
        raw_copy(part).wait()
        flat[...] = raw[part].astype(jnp.float32).reshape(rows * heads, width)
        for h in range(heads):
            own[part, h] = flat[pl.ds(h, rows, stride=heads), :].astype(own.dtype)
        if part == 0:
            pl.semaphore_wait(
                barrier, 1 + has_up.astype(jnp.int32) + has_down.astype(jnp.int32)
            )
            for c in range(PIECES):
                launch(c)

    def launch_rest(c, carry):
        launch(c)
        return carry

    lax.fori_loop(PIECES, chunks, launch_rest, 0)

    for h in range(heads):
        q_copy(h).start()

    @pl.when(me < 2)
    def _():
        win[:, :, 0:rows, :] = jnp.zeros((2, heads, rows, width), win.dtype)

    @pl.when(me < 1)
    def _():
        win[:, :, rows : 2 * rows, :] = jnp.zeros((2, heads, rows, width), win.dtype)

    row_token = lax.broadcasted_iota(jnp.int32, (BLOCK, group, LANES), 0)
    lane = lax.broadcasted_iota(jnp.int32, (BLOCK, group, LANES), 2)
    hot[...] = (
        jnp.where(row_token == lane, 1.0, 0.0).reshape(BLOCK * group, LANES).astype(hot.dtype)
    )

    def fill_bias(block, carry):
        base = me * rows
        token = base + block * BLOCK + lax.broadcasted_iota(jnp.int32, (1, LANES), 1)
        first = jnp.zeros((1, LANES), jnp.int32)
        end = jnp.int32(0)
        for d in range(lengths.shape[1]):
            end = end + lengths[0, d]
            first = jnp.where(token >= end, end, first)
        key = base + lax.broadcasted_iota(jnp.int32, (rows, LANES), 0)
        allowed = (key >= first) & (key <= token)
        bias_own[block] = jnp.where(allowed, 0.0, MASKED).astype(bias_own.dtype)
        key = base - 2 * rows + lax.broadcasted_iota(jnp.int32, (2 * rows, LANES), 0)
        bias_win[block] = jnp.where(key >= first, 0.0, MASKED).astype(bias_win.dtype)
        return carry

    lax.fori_loop(0, blocks, fill_bias, 0)

    def queries_of(h, block):
        at = pl.ds(pl.multiple_of(block * BLOCK, BLOCK), BLOCK)
        q = qbuf[h, at].reshape(BLOCK * group, width)
        return jnp.concatenate([q, hot[...]], axis=1)

    def score_own(h, block, span, scores, tops):
        score_tile(
            queries_of(h, block), own[0, h, 0:span, :], bias_own[block, 0:span], None, scores, tops
        )

    def value_own(h, block, span, scores, tops):
        at = h * blocks + block
        state[at] = weigh(scores, tops, own[1, h, 0:span, :])
        state_top[at] = tops[...]

    def score_win(h, block, start, scores, tops):
        before = state_top[h * blocks + block]
        score_tile(
            queries_of(h, block), win[0, h, start:, :], bias_win[block, start:], before, scores, tops
        )

    def value_win(h, block, start, scores, tops):
        at = h * blocks + block
        total = weigh(scores, tops, win[1, h, start:, :])
        result = merged(total, state[at], state_top[at], tops[...])
        out[
            pl.ds(pl.multiple_of(block * BLOCK, BLOCK), BLOCK),
            pl.ds(pl.multiple_of(h * group, group), group),
            :,
        ] = result.reshape(BLOCK, group, width).astype(out.dtype)

    pairs = heads * half
    near_half, far_half = rows // 2, 0

    def pair_at(index, most):
        index = jnp.minimum(index, most - 1)
        return lax.div(index, half), lax.rem(index, half)

    for h in range(heads):
        q_copy(h).wait()

    score_own(0, 0, rows // 2, scores_a, tops_a)

    def own_lap(lap, carry):
        forward(lax.div(3 * lap, 2))

        @pl.when(lax.rem(lap, 2) == 1)
        def _():
            forward(lax.div(3 * lap, 2) + 1)

        for i in range(half):
            h, j = pair_at(lap * half + i, pairs)
            next_h, next_j = pair_at(lap * half + i + 1, pairs)
            score_own(h, j + half, rows, scores_b, tops_b)
            value_own(h, j, rows // 2, scores_a, tops_a)
            score_own(next_h, next_j, rows // 2, scores_a, tops_a)
            value_own(h, j + half, rows, scores_b, tops_b)
        return carry

    lax.fori_loop(0, heads, own_lap, 0)

    arrive(0, 0)
    score_win(0, 0, far_half, scores_a, tops_a)
    laps = half // STRIDE
    early = 3 * heads // 2
    last = heads - 1

    def win_lap(lap, carry):
        h, part = lax.div(lap, laps), lax.rem(lap, laps)

        first = early + lax.div(3 * lap, 2)
        forward_some(first, jnp.minimum(early + lax.div(3 * lap + 3, 2), chunks))

        @pl.when(part == 0)
        def _():
            arrive(h, 1)

        @pl.when((part == laps - 1) & (h + 1 < last))
        def _():
            arrive(h + 1, 0)

        for i in range(STRIDE):
            h, j = pair_at(lap * STRIDE + i, last * half)
            next_h, next_j = pair_at(lap * STRIDE + i + 1, last * half)
            score_win(h, j + half, near_half, scores_b, tops_b)
            value_win(h, j, far_half, scores_a, tops_a)
            score_win(next_h, next_j, far_half, scores_a, tops_a)
            value_win(h, j + half, near_half, scores_b, tops_b)
        return carry

    lax.fori_loop(0, last * laps, win_lap, 0)

    for c in range(early + 3 * last * laps // 2, chunks):
        forward(c)
    last_q[...] = qbuf[last]
    last_state[...] = state[last * blocks :]
    last_top[...] = state_top[last * blocks :]
    for part in range(2):
        arrive(last, part)
        last_win[part] = win[part, last]

    for c in range(chunks):

        @pl.when(has_up)
        def _():
            far_copy(c).wait_send()

        @pl.when(even | has_down)
        def _():
            near_copy(c).wait_send()


def finish_kernel(lengths, done, win, qbuf, hot, bias_win, state, state_top, out_hbm, obuf, scores_a,
                  scores_b, tops_a, tops_b, done_sem, osem):
    rows, group, width = qbuf.shape
    blocks = rows // BLOCK
    half = blocks // 2
    laps = half // STRIDE
    ahead = done.shape[1]
    base = lax.axis_index("ctx") * rows

    ready = pltpu.make_async_copy(done, out_hbm.at[:, 0:ahead, :], done_sem)
    ready.start()

    def o_copy(block):
        at = pl.ds(pl.multiple_of(block * BLOCK, BLOCK), STRIDE * BLOCK)
        return pltpu.make_async_copy(
            obuf.at[at], out_hbm.at[at, ahead:, :], osem.at[lax.div(block, STRIDE)]
        )

    def first_of(token):
        first, end = jnp.int32(0), jnp.int32(0)
        for d in range(lengths.shape[1]):
            end = end + lengths[0, d]
            first = jnp.where(token >= end, end, first)
        return first

    def at_rows(block):
        return pl.ds(pl.multiple_of(block * BLOCK, BLOCK), BLOCK)

    def score(block, start, scores, tops):
        q = qbuf[at_rows(block)].reshape(BLOCK * group, width)
        q = jnp.concatenate([q, hot[...]], axis=1)
        keys, before = win[0, start:, :], state_top[block]
        score_tile(q, keys, bias_win[block, start:], before, scores, tops)

    def put(block, result):
        obuf[at_rows(block)] = result.reshape(BLOCK, group, width).astype(obuf.dtype)

    def value(block, start, scores, tops):
        total = weigh(scores, tops, win[1, start:, :])
        put(block, merged(total, state[block], state_top[block], tops[...]))

    def leave(lap):
        o_copy(lap * STRIDE).start()
        o_copy(lap * STRIDE + half).start()

    first = first_of(base)
    reach = first - (base - 2 * rows)
    busy = jnp.where(
        first >= base, 0, jnp.where(first_of(base + STRIDE * BLOCK) >= base, 1, laps)
    )

    for low, high, edge in ((-rows, rows // 2, 0), (rows // 2, rows, rows // 2), (rows, 2 * rows, rows)):

        @pl.when((reach >= low) & (reach < high))
        def _():
            far, near = edge, max(edge, rows // 2)
            score(0, far, scores_a, tops_a)

            def lap_of(lap, carry):
                for i in range(STRIDE):
                    j = lap * STRIDE + i
                    later = jnp.minimum(j + 1, half - 1)
                    score(j + half, near, scores_b, tops_b)
                    value(j, far, scores_a, tops_a)
                    score(later, far, scores_a, tops_a)
                    value(j + half, near, scores_b, tops_b)
                leave(lap)
                return carry

            lax.fori_loop(0, busy, lap_of, 0)

    def rest(lap, carry):
        for i in range(STRIDE):
            for block in (lap * STRIDE + i, lap * STRIDE + i + half):
                put(block, normalized(state[block]))
        leave(lap)
        return carry

    lax.fori_loop(busy, laps, rest, 0)

    for lap in range(2 * laps):
        o_copy(lap * STRIDE).wait()
    ready.wait()


def body(count, queries, keys, values, doc_lengths):
    rows, query_heads, width = queries.shape
    heads = keys.shape[1]
    group = query_heads // heads
    blocks = rows // BLOCK
    chunks = 2 * PIECES * heads
    any_space = pl.BlockSpec(memory_space=pl.ANY)
    smem = pl.BlockSpec(memory_space=pltpu.SMEM)
    vmem = pl.BlockSpec(memory_space=pltpu.VMEM)
    work = [
        pltpu.VMEM((BLOCK * group, 2 * rows), jnp.float32),
        pltpu.VMEM((BLOCK * group, 3 * rows // 2), jnp.float32),
        pltpu.VMEM((BLOCK * group, LANES), jnp.float32),
        pltpu.VMEM((BLOCK * group, LANES), jnp.float32),
    ]
    carried = pl.pallas_call(
        functools.partial(gather_kernel, count),
        out_shape=[
            pltpu.VMEM((rows, query_heads - group, width), queries.dtype),
            pltpu.VMEM((2, 2 * rows, width), keys.dtype),
            pltpu.VMEM((rows, group, width), queries.dtype),
            pltpu.VMEM((BLOCK * group, LANES), queries.dtype),
            pltpu.VMEM((blocks, 2 * rows, LANES), queries.dtype),
            pltpu.VMEM((blocks, BLOCK * group, 2 * width), jnp.float32),
            pltpu.VMEM((blocks, BLOCK * group, LANES), jnp.float32),
        ],
        in_specs=[smem, any_space, any_space, any_space],
        out_specs=[vmem] * 7,
        scratch_shapes=[
            pltpu.VMEM((2, heads, rows, width), keys.dtype),
            pltpu.VMEM((2, heads, 2 * rows, width), keys.dtype),
            pltpu.VMEM((heads, rows, group, width), queries.dtype),
            pltpu.VMEM((heads * blocks, BLOCK * group, 2 * width), jnp.float32),
            pltpu.VMEM((heads * blocks, BLOCK * group, LANES), jnp.float32),
            pltpu.VMEM((2, rows, heads, width), keys.dtype),
            pltpu.VMEM((rows * heads, width), jnp.float32),
            pltpu.VMEM((blocks, rows, LANES), queries.dtype),
            *work,
            pltpu.SemaphoreType.DMA((heads,)),
            pltpu.SemaphoreType.DMA((2,)),
            pltpu.SemaphoreType.DMA((chunks,)),
            pltpu.SemaphoreType.DMA((chunks,)),
            pltpu.SemaphoreType.DMA((chunks,)),
            pltpu.SemaphoreType.DMA((chunks,)),
        ],
        compiler_params=pltpu.CompilerParams(
            collective_id=0, has_side_effects=True, vmem_limit_bytes=44 * 1024 * 1024
        ),
    )(doc_lengths, queries, keys, values)
    return pl.pallas_call(
        finish_kernel,
        out_shape=jax.ShapeDtypeStruct(queries.shape, queries.dtype),
        in_specs=[smem] + [vmem] * 7,
        out_specs=any_space,
        scratch_shapes=[
            pltpu.VMEM((rows, group, width), queries.dtype),
            *work,
            pltpu.SemaphoreType.DMA,
            pltpu.SemaphoreType.DMA((blocks // STRIDE,)),
        ],
        compiler_params=pltpu.CompilerParams(vmem_limit_bytes=12 * 1024 * 1024),
    )(doc_lengths, *carried)


def solution(mesh):
    placed = (
        P(("dp", "ctx"), None, None),
        P(("dp", "ctx"), None, None),
        P(("dp", "ctx"), None, None),
        P("dp", None),
    )
    return jax.shard_map(
        functools.partial(body, mesh.shape["ctx"]),
        mesh=mesh,
        in_specs=placed,
        out_specs=P(("dp", "ctx"), None, None),
        check_vma=False,
    )
```

```python
import functools
import math

import jax
import jax.numpy as jnp
from jax import lax
from jax.experimental import pallas as pl
from jax.experimental.pallas import tpu as pltpu
from jax.sharding import PartitionSpec as P

LANES = 128
BLOCK = 64
PIECES = 2
STRIDE = 2
MASKED = -1e30
MESH = pl.DeviceIdType.MESH


def product(q, keys):
    return lax.dot_general(q, keys, (((1,), (1,)), ((), ())), preferred_element_type=jnp.float32)


def rate_of(width):
    return math.log2(math.e) / math.sqrt(width)


def weigh(scores, tops, values):
    span, width = values.shape
    ones = jnp.ones((span, LANES), values.dtype)
    top = jnp.concatenate([tops[...]] * (span // LANES), axis=1)
    weights = jnp.exp2((scores[:, 0:span] - top) * rate_of(width)).astype(values.dtype)
    return jnp.dot(
        weights, jnp.concatenate([values, ones], axis=1), preferred_element_type=jnp.float32
    )


def score_tile(q, keys, bias, before, scores, tops):
    found = product(q, jnp.concatenate([keys, bias], axis=1))
    scores[:, 0 : keys.shape[0]] = found
    best = jnp.broadcast_to(jnp.max(found, axis=1, keepdims=True), tops.shape)
    tops[...] = best if before is None else jnp.maximum(best, before)


def normalized(total):
    width = total.shape[1] // 2
    return total[:, :width] / total[:, width:]


def merged(total, state, state_top, tops):
    scale = jnp.exp2((state_top - tops) * rate_of(total.shape[1] // 2))
    return normalized(total + state * jnp.concatenate([scale, scale], axis=1))


def gather_kernel(count, lengths, q_hbm, k_hbm, v_hbm, out, last_win, last_q, hot, bias_win,
                  last_state, last_top, own, win, qbuf, state, state_top, raw, flat, bias_own,
                  scores_a, scores_b, tops_a, tops_b, spare, qsem, rawsem, far_send,
                  far_recv, near_send, near_recv, spare_sem):
    rows, heads, width = k_hbm.shape
    group = q_hbm.shape[1] // heads
    blocks = rows // BLOCK
    half = blocks // 2
    piece_rows = rows // PIECES
    per_head = 2 * PIECES
    chunks = per_head * heads
    me = lax.axis_index("ctx")
    odd = lax.rem(me, 2) == 1
    even = jnp.logical_not(odd)
    partner = jnp.where(odd, me - 1, me + 1)
    has_up = me + 2 < count
    has_down = me >= 2
    lends = odd & (me + 1 < count)
    hands = even & has_up

    barrier = pltpu.get_barrier_semaphore()

    def greet(other):
        pl.semaphore_signal(barrier, inc=1, device_id={"ctx": other}, device_id_type=MESH)

    def q_copy(h):
        return pltpu.make_async_copy(
            q_hbm.at[:, pl.ds(h * group, group), :], qbuf.at[h], qsem.at[h]
        )

    def raw_copy(part):
        return pltpu.make_async_copy((k_hbm, v_hbm)[part], raw.at[part], rawsem.at[part])

    def place(c):
        h, rest = lax.div(c, per_head), lax.rem(c, per_head)
        part, piece = lax.div(rest, PIECES), lax.rem(rest, PIECES)
        return part, h, pl.multiple_of(piece * piece_rows, piece_rows)

    def far_copy(c):
        part, h, first = place(c)
        return pltpu.make_async_remote_copy(
            src_ref=own.at[part, h, pl.ds(first, piece_rows), :],
            dst_ref=win.at[part, h, pl.ds(first, piece_rows), :],
            send_sem=far_send.at[c],
            recv_sem=far_recv.at[c],
            device_id={"ctx": me + 2},
            device_id_type=MESH,
        )

    def near_copy(c):
        part, h, first = place(c)
        return pltpu.make_async_remote_copy(
            src_ref=own.at[part, h, pl.ds(first, piece_rows), :],
            dst_ref=win.at[part, h, pl.ds(rows + first, piece_rows), :],
            send_sem=near_send.at[c],
            recv_sem=near_recv.at[c],
            device_id={"ctx": partner},
            device_id_type=MESH,
        )

    def relay_copy(c):
        part, h, first = place(c)
        return pltpu.make_async_remote_copy(
            src_ref=win.at[part, h, pl.ds(first, piece_rows), :],
            dst_ref=win.at[part, h, pl.ds(rows + first, piece_rows), :],
            send_sem=near_send.at[c],
            recv_sem=near_recv.at[c],
            device_id={"ctx": partner},
            device_id_type=MESH,
        )

    def spare_copy():
        part, h, first = place(chunks - 1)
        return pltpu.make_async_remote_copy(
            src_ref=own.at[part, h, pl.ds(first, piece_rows), :],
            dst_ref=spare,
            send_sem=spare_sem.at[0],
            recv_sem=spare_sem.at[1],
            device_id={"ctx": partner},
            device_id_type=MESH,
        )

    def hand_copy():
        part, h, first = place(chunks - 1)
        return pltpu.make_async_remote_copy(
            src_ref=spare,
            dst_ref=win.at[part, h, pl.ds(rows + first, piece_rows), :],
            send_sem=spare_sem.at[0],
            recv_sem=near_recv.at[chunks - 1],
            device_id={"ctx": me + 2},
            device_id_type=MESH,
        )

    def launch(c):
        @pl.when(has_up)
        def _():
            far_copy(c).start()

        @pl.when(even)
        def _():
            near_copy(c).start()

    def forward(c):
        @pl.when(odd & has_down)
        def _():
            far_copy(c).wait_recv()

            @pl.when(c < chunks - 1)
            def _():
                relay_copy(c).start()

    def forward_some(first, limit):
        for c in (first, first + 1):

            @pl.when(c < limit)
            def _():
                forward(c)

    def arrive(h, part):
        for piece in range(PIECES):
            c = h * per_head + part * PIECES + piece

            @pl.when(even & has_down)
            def _():
                far_copy(c).wait_recv()

            @pl.when(me >= 1)
            def _():
                near_copy(c).wait_recv()

    greet(partner)

    @pl.when(has_up)
    def _():
        greet(me + 2)

    @pl.when(has_down)
    def _():
        greet(me - 2)

    for part in range(2):
        raw_copy(part).start()
    for part in range(2):
        raw_copy(part).wait()
        flat[...] = raw[part].astype(jnp.float32).reshape(rows * heads, width)
        for h in range(heads):
            own[part, h] = flat[pl.ds(h, rows, stride=heads), :].astype(own.dtype)
        if part == 0:
            pl.semaphore_wait(
                barrier, 1 + has_up.astype(jnp.int32) + has_down.astype(jnp.int32)
            )
            for c in range(PIECES):
                launch(c)

    @pl.when(lends)
    def _():
        spare_copy().start()

    def launch_rest(c, carry):
        launch(c)
        return carry

    lax.fori_loop(PIECES, chunks, launch_rest, 0)

    for h in range(heads):
        q_copy(h).start()

    @pl.when(me < 2)
    def _():
        win[:, :, 0:rows, :] = jnp.zeros((2, heads, rows, width), win.dtype)

    @pl.when(me < 1)
    def _():
        win[:, :, rows : 2 * rows, :] = jnp.zeros((2, heads, rows, width), win.dtype)

    row_token = lax.broadcasted_iota(jnp.int32, (BLOCK, group, LANES), 0)
    lane = lax.broadcasted_iota(jnp.int32, (BLOCK, group, LANES), 2)
    hot[...] = (
        jnp.where(row_token == lane, 1.0, 0.0).reshape(BLOCK * group, LANES).astype(hot.dtype)
    )

    def fill_bias(block, carry):
        base = me * rows
        token = base + block * BLOCK + lax.broadcasted_iota(jnp.int32, (1, LANES), 1)
        first = jnp.zeros((1, LANES), jnp.int32)
        end = jnp.int32(0)
        for d in range(lengths.shape[1]):
            end = end + lengths[0, d]
            first = jnp.where(token >= end, end, first)
        key = base + lax.broadcasted_iota(jnp.int32, (rows, LANES), 0)
        allowed = (key >= first) & (key <= token)
        bias_own[block] = jnp.where(allowed, 0.0, MASKED).astype(bias_own.dtype)
        key = base - 2 * rows + lax.broadcasted_iota(jnp.int32, (2 * rows, LANES), 0)
        bias_win[block] = jnp.where(key >= first, 0.0, MASKED).astype(bias_win.dtype)
        return carry

    lax.fori_loop(0, blocks - 1, fill_bias, 0)
    forward(0)

    @pl.when(hands)
    def _():
        spare_copy().wait_recv()
        hand_copy().start()

    lax.fori_loop(blocks - 1, blocks, fill_bias, 0)

    def queries_of(h, block):
        at = pl.ds(pl.multiple_of(block * BLOCK, BLOCK), BLOCK)
        q = qbuf[h, at].reshape(BLOCK * group, width)
        return jnp.concatenate([q, hot[...]], axis=1)

    def score_own(h, block, span, scores, tops):
        score_tile(
            queries_of(h, block), own[0, h, 0:span, :], bias_own[block, 0:span], None, scores, tops
        )

    def value_own(h, block, span, scores, tops):
        at = h * blocks + block
        state[at] = weigh(scores, tops, own[1, h, 0:span, :])
        state_top[at] = tops[...]

    def score_win(h, block, start, scores, tops):
        before = state_top[h * blocks + block]
        score_tile(
            queries_of(h, block), win[0, h, start:, :], bias_win[block, start:], before, scores, tops
        )

    def value_win(h, block, start, scores, tops):
        at = h * blocks + block
        total = weigh(scores, tops, win[1, h, start:, :])
        result = merged(total, state[at], state_top[at], tops[...])
        out[
            pl.ds(pl.multiple_of(block * BLOCK, BLOCK), BLOCK),
            pl.ds(pl.multiple_of(h * group, group), group),
            :,
        ] = result.reshape(BLOCK, group, width).astype(out.dtype)

    pairs = heads * half
    near_half, far_half = rows // 2, 0

    def pair_at(index, most):
        index = jnp.minimum(index, most - 1)
        return lax.div(index, half), lax.rem(index, half)

    for h in range(heads):
        q_copy(h).wait()

    score_own(0, 0, rows // 2, scores_a, tops_a)

    def own_lap(lap, carry):
        forward_some(jnp.maximum(lax.div(3 * lap, 2), 1), lax.div(3 * lap + 3, 2))

        for i in range(half):
            h, j = pair_at(lap * half + i, pairs)
            next_h, next_j = pair_at(lap * half + i + 1, pairs)
            score_own(h, j + half, rows, scores_b, tops_b)
            value_own(h, j, rows // 2, scores_a, tops_a)
            score_own(next_h, next_j, rows // 2, scores_a, tops_a)
            value_own(h, j + half, rows, scores_b, tops_b)
        return carry

    lax.fori_loop(0, heads, own_lap, 0)

    arrive(0, 0)
    score_win(0, 0, far_half, scores_a, tops_a)
    laps = half // STRIDE
    early = 3 * heads // 2
    last = heads - 1

    def win_lap(lap, carry):
        h, part = lax.div(lap, laps), lax.rem(lap, laps)

        first = early + lax.div(3 * lap, 2)
        forward_some(first, jnp.minimum(early + lax.div(3 * lap + 3, 2), chunks))

        @pl.when(part == 0)
        def _():
            arrive(h, 1)

        @pl.when((part == laps - 1) & (h + 1 < last))
        def _():
            arrive(h + 1, 0)

        for i in range(STRIDE):
            h, j = pair_at(lap * STRIDE + i, last * half)
            next_h, next_j = pair_at(lap * STRIDE + i + 1, last * half)
            score_win(h, j + half, near_half, scores_b, tops_b)
            value_win(h, j, far_half, scores_a, tops_a)
            score_win(next_h, next_j, far_half, scores_a, tops_a)
            value_win(h, j + half, near_half, scores_b, tops_b)
        return carry

    lax.fori_loop(0, last * laps, win_lap, 0)

    for c in range(early + 3 * last * laps // 2, chunks):
        forward(c)
    last_q[...] = qbuf[last]
    last_state[...] = state[last * blocks :]
    last_top[...] = state_top[last * blocks :]
    for part in range(2):
        arrive(last, part)
        last_win[part] = win[part, last]

    for c in range(chunks):

        @pl.when(has_up)
        def _():
            far_copy(c).wait_send()

        @pl.when(even | (has_down if c < chunks - 1 else False))
        def _():
            near_copy(c).wait_send()

    @pl.when(lends | hands)
    def _():
        spare_copy().wait_send()


def finish_kernel(lengths, done, win, qbuf, hot, bias_win, state, state_top, out_hbm, obuf, scores_a,
                  scores_b, tops_a, tops_b, done_sem, osem):
    rows, group, width = qbuf.shape
    blocks = rows // BLOCK
    half = blocks // 2
    laps = half // STRIDE
    ahead = done.shape[1]
    base = lax.axis_index("ctx") * rows

    ready = pltpu.make_async_copy(done, out_hbm.at[:, 0:ahead, :], done_sem)
    ready.start()

    def o_copy(block):
        at = pl.ds(pl.multiple_of(block * BLOCK, BLOCK), STRIDE * BLOCK)
        return pltpu.make_async_copy(
            obuf.at[at], out_hbm.at[at, ahead:, :], osem.at[lax.div(block, STRIDE)]
        )

    def first_of(token):
        first, end = jnp.int32(0), jnp.int32(0)
        for d in range(lengths.shape[1]):
            end = end + lengths[0, d]
            first = jnp.where(token >= end, end, first)
        return first

    def at_rows(block):
        return pl.ds(pl.multiple_of(block * BLOCK, BLOCK), BLOCK)

    def score(block, start, scores, tops):
        q = qbuf[at_rows(block)].reshape(BLOCK * group, width)
        q = jnp.concatenate([q, hot[...]], axis=1)
        keys, before = win[0, start:, :], state_top[block]
        score_tile(q, keys, bias_win[block, start:], before, scores, tops)

    def put(block, result):
        obuf[at_rows(block)] = result.reshape(BLOCK, group, width).astype(obuf.dtype)

    def value(block, start, scores, tops):
        total = weigh(scores, tops, win[1, start:, :])
        put(block, merged(total, state[block], state_top[block], tops[...]))

    def leave(lap):
        o_copy(lap * STRIDE).start()
        o_copy(lap * STRIDE + half).start()

    first = first_of(base)
    reach = first - (base - 2 * rows)
    busy = jnp.where(
        first >= base, 0, jnp.where(first_of(base + STRIDE * BLOCK) >= base, 1, laps)
    )

    for low, high, edge in ((-rows, rows // 2, 0), (rows // 2, rows, rows // 2), (rows, 2 * rows, rows)):

        @pl.when((reach >= low) & (reach < high))
        def _():
            far, near = edge, max(edge, rows // 2)
            score(0, far, scores_a, tops_a)

            def lap_of(lap, carry):
                for i in range(STRIDE):
                    j = lap * STRIDE + i
                    later = jnp.minimum(j + 1, half - 1)
                    score(j + half, near, scores_b, tops_b)
                    value(j, far, scores_a, tops_a)
                    score(later, far, scores_a, tops_a)
                    value(j + half, near, scores_b, tops_b)
                leave(lap)
                return carry

            lax.fori_loop(0, busy, lap_of, 0)

    def rest(lap, carry):
        for i in range(STRIDE):
            for block in (lap * STRIDE + i, lap * STRIDE + i + half):
                put(block, normalized(state[block]))
        leave(lap)
        return carry

    lax.fori_loop(busy, laps, rest, 0)

    for lap in range(2 * laps):
        o_copy(lap * STRIDE).wait()
    ready.wait()


def body(count, queries, keys, values, doc_lengths):
    rows, query_heads, width = queries.shape
    heads = keys.shape[1]
    group = query_heads // heads
    blocks = rows // BLOCK
    chunks = 2 * PIECES * heads
    any_space = pl.BlockSpec(memory_space=pl.ANY)
    smem = pl.BlockSpec(memory_space=pltpu.SMEM)
    vmem = pl.BlockSpec(memory_space=pltpu.VMEM)
    work = [
        pltpu.VMEM((BLOCK * group, 2 * rows), jnp.float32),
        pltpu.VMEM((BLOCK * group, 3 * rows // 2), jnp.float32),
        pltpu.VMEM((BLOCK * group, LANES), jnp.float32),
        pltpu.VMEM((BLOCK * group, LANES), jnp.float32),
    ]
    carried = pl.pallas_call(
        functools.partial(gather_kernel, count),
        out_shape=[
            pltpu.VMEM((rows, query_heads - group, width), queries.dtype),
            pltpu.VMEM((2, 2 * rows, width), keys.dtype),
            pltpu.VMEM((rows, group, width), queries.dtype),
            pltpu.VMEM((BLOCK * group, LANES), queries.dtype),
            pltpu.VMEM((blocks, 2 * rows, LANES), queries.dtype),
            pltpu.VMEM((blocks, BLOCK * group, 2 * width), jnp.float32),
            pltpu.VMEM((blocks, BLOCK * group, LANES), jnp.float32),
        ],
        in_specs=[smem, any_space, any_space, any_space],
        out_specs=[vmem] * 7,
        scratch_shapes=[
            pltpu.VMEM((2, heads, rows, width), keys.dtype),
            pltpu.VMEM((2, heads, 2 * rows, width), keys.dtype),
            pltpu.VMEM((heads, rows, group, width), queries.dtype),
            pltpu.VMEM((heads * blocks, BLOCK * group, 2 * width), jnp.float32),
            pltpu.VMEM((heads * blocks, BLOCK * group, LANES), jnp.float32),
            pltpu.VMEM((2, rows, heads, width), keys.dtype),
            pltpu.VMEM((rows * heads, width), jnp.float32),
            pltpu.VMEM((blocks, rows, LANES), queries.dtype),
            *work,
            pltpu.VMEM((rows // PIECES, width), keys.dtype),
            pltpu.SemaphoreType.DMA((heads,)),
            pltpu.SemaphoreType.DMA((2,)),
            pltpu.SemaphoreType.DMA((chunks,)),
            pltpu.SemaphoreType.DMA((chunks,)),
            pltpu.SemaphoreType.DMA((chunks,)),
            pltpu.SemaphoreType.DMA((chunks,)),
            pltpu.SemaphoreType.DMA((2,)),
        ],
        compiler_params=pltpu.CompilerParams(
            collective_id=0, has_side_effects=True, vmem_limit_bytes=44 * 1024 * 1024
        ),
    )(doc_lengths, queries, keys, values)
    return pl.pallas_call(
        finish_kernel,
        out_shape=jax.ShapeDtypeStruct(queries.shape, queries.dtype),
        in_specs=[smem] + [vmem] * 7,
        out_specs=any_space,
        scratch_shapes=[
            pltpu.VMEM((rows, group, width), queries.dtype),
            *work,
            pltpu.SemaphoreType.DMA,
            pltpu.SemaphoreType.DMA((blocks // STRIDE,)),
        ],
        compiler_params=pltpu.CompilerParams(vmem_limit_bytes=12 * 1024 * 1024),
    )(doc_lengths, *carried)


def solution(mesh):
    placed = (
        P(("dp", "ctx"), None, None),
        P(("dp", "ctx"), None, None),
        P(("dp", "ctx"), None, None),
        P("dp", None),
    )
    return jax.shard_map(
        functools.partial(body, mesh.shape["ctx"]),
        mesh=mesh,
        in_specs=placed,
        out_specs=P(("dp", "ctx"), None, None),
        check_vma=False,
    )
```

```python
import functools
import math

import jax
import jax.numpy as jnp
from jax import lax
from jax.experimental import pallas as pl
from jax.experimental.pallas import tpu as pltpu
from jax.sharding import PartitionSpec as P

LANES = 128
BLOCK = 64
PIECES = 2
STRIDE = 2
MASKED = -1e30
MESH = pl.DeviceIdType.MESH


def product(q, keys):
    return lax.dot_general(q, keys, (((1,), (1,)), ((), ())), preferred_element_type=jnp.float32)


def rate_of(width):
    return math.log2(math.e) / math.sqrt(width)


def weigh(scores, tops, values):
    span, width = values.shape
    ones = jnp.ones((span, LANES), values.dtype)
    top = jnp.concatenate([tops[...]] * (span // LANES), axis=1)
    weights = jnp.exp2((scores[:, 0:span] - top) * rate_of(width)).astype(values.dtype)
    return jnp.dot(
        weights, jnp.concatenate([values, ones], axis=1), preferred_element_type=jnp.float32
    )


def score_tile(q, keys, bias, before, scores, tops):
    found = product(q, jnp.concatenate([keys, bias], axis=1))
    scores[:, 0 : keys.shape[0]] = found
    best = jnp.broadcast_to(jnp.max(found, axis=1, keepdims=True), tops.shape)
    tops[...] = best if before is None else jnp.maximum(best, before)


def normalized(total):
    width = total.shape[1] // 2
    return total[:, :width] / total[:, width:]


def merged(total, state, state_top, tops):
    scale = jnp.exp2((state_top - tops) * rate_of(total.shape[1] // 2))
    return normalized(total + state * jnp.concatenate([scale, scale], axis=1))


def gather_kernel(count, lengths, q_hbm, k_hbm, v_hbm, out, last_win, last_q, hot, bias_win,
                  last_state, last_top, own, win, qbuf, state, state_top, raw, flat, bias_own,
                  scores_a, scores_b, tops_a, tops_b, spare, qsem, rawsem, far_send,
                  far_recv, near_send, near_recv, spare_sem):
    rows, heads, width = k_hbm.shape
    group = q_hbm.shape[1] // heads
    blocks = rows // BLOCK
    half = blocks // 2
    piece_rows = rows // PIECES
    per_head = 2 * PIECES
    chunks = per_head * heads
    me = lax.axis_index("ctx")
    odd = lax.rem(me, 2) == 1
    even = jnp.logical_not(odd)
    partner = jnp.where(odd, me - 1, me + 1)
    has_up = me + 2 < count
    has_down = me >= 2
    lends = odd & (me + 1 < count)
    hands = even & has_up

    barrier = pltpu.get_barrier_semaphore()

    def greet(other):
        pl.semaphore_signal(barrier, inc=1, device_id={"ctx": other}, device_id_type=MESH)

    def q_copy(h):
        return pltpu.make_async_copy(
            q_hbm.at[:, pl.ds(h * group, group), :], qbuf.at[h], qsem.at[h]
        )

    def raw_copy(part):
        return pltpu.make_async_copy((k_hbm, v_hbm)[part], raw.at[part], rawsem.at[part])

    def place(c):
        h, rest = lax.div(c, per_head), lax.rem(c, per_head)
        part, piece = lax.div(rest, PIECES), lax.rem(rest, PIECES)
        return part, h, pl.multiple_of(piece * piece_rows, piece_rows)

    def far_copy(c):
        part, h, first = place(c)
        return pltpu.make_async_remote_copy(
            src_ref=own.at[part, h, pl.ds(first, piece_rows), :],
            dst_ref=win.at[part, h, pl.ds(first, piece_rows), :],
            send_sem=far_send.at[c],
            recv_sem=far_recv.at[c],
            device_id={"ctx": me + 2},
            device_id_type=MESH,
        )

    def near_copy(c):
        part, h, first = place(c)
        return pltpu.make_async_remote_copy(
            src_ref=own.at[part, h, pl.ds(first, piece_rows), :],
            dst_ref=win.at[part, h, pl.ds(rows + first, piece_rows), :],
            send_sem=near_send.at[c],
            recv_sem=near_recv.at[c],
            device_id={"ctx": partner},
            device_id_type=MESH,
        )

    def relay_copy(c):
        part, h, first = place(c)
        return pltpu.make_async_remote_copy(
            src_ref=win.at[part, h, pl.ds(first, piece_rows), :],
            dst_ref=win.at[part, h, pl.ds(rows + first, piece_rows), :],
            send_sem=near_send.at[c],
            recv_sem=near_recv.at[c],
            device_id={"ctx": partner},
            device_id_type=MESH,
        )

    def spare_copy():
        part, h, first = place(chunks - 1)
        return pltpu.make_async_remote_copy(
            src_ref=own.at[part, h, pl.ds(first, piece_rows), :],
            dst_ref=spare,
            send_sem=spare_sem.at[0],
            recv_sem=spare_sem.at[1],
            device_id={"ctx": partner},
            device_id_type=MESH,
        )

    def hand_copy():
        part, h, first = place(chunks - 1)
        return pltpu.make_async_remote_copy(
            src_ref=spare,
            dst_ref=win.at[part, h, pl.ds(rows + first, piece_rows), :],
            send_sem=spare_sem.at[0],
            recv_sem=near_recv.at[chunks - 1],
            device_id={"ctx": me + 2},
            device_id_type=MESH,
        )

    def launch(c):
        @pl.when(has_up)
        def _():
            far_copy(c).start()

        @pl.when(even)
        def _():
            near_copy(c).start()

    def forward(c):
        @pl.when(odd & has_down)
        def _():
            far_copy(c).wait_recv()

            @pl.when(c < chunks - 1)
            def _():
                relay_copy(c).start()

    def forward_some(first, limit):
        for c in (first, first + 1):

            @pl.when(c < limit)
            def _():
                forward(c)

    def arrive(h, part):
        for piece in range(PIECES):
            c = h * per_head + part * PIECES + piece

            @pl.when(even & has_down)
            def _():
                far_copy(c).wait_recv()

            @pl.when(me >= 1)
            def _():
                near_copy(c).wait_recv()

    greet(partner)

    @pl.when(has_up)
    def _():
        greet(me + 2)

    @pl.when(has_down)
    def _():
        greet(me - 2)

    for part in range(2):
        raw_copy(part).start()
    for part in range(2):
        raw_copy(part).wait()
        flat[...] = raw[part].astype(jnp.float32).reshape(rows * heads, width)
        for h in range(heads):
            own[part, h] = flat[pl.ds(h, rows, stride=heads), :].astype(own.dtype)
        if part == 0:
            pl.semaphore_wait(
                barrier, 1 + has_up.astype(jnp.int32) + has_down.astype(jnp.int32)
            )
            for c in range(PIECES):
                launch(c)

    @pl.when(lends)
    def _():
        spare_copy().start()

    def launch_rest(c, carry):
        launch(c)
        return carry

    lax.fori_loop(PIECES, chunks, launch_rest, 0)

    for h in range(heads):
        q_copy(h).start()

    @pl.when(me < 2)
    def _():
        win[:, :, 0:rows, :] = jnp.zeros((2, heads, rows, width), win.dtype)

    @pl.when(me < 1)
    def _():
        win[:, :, rows : 2 * rows, :] = jnp.zeros((2, heads, rows, width), win.dtype)

    row_token = lax.broadcasted_iota(jnp.int32, (BLOCK, group, LANES), 0)
    lane = lax.broadcasted_iota(jnp.int32, (BLOCK, group, LANES), 2)
    hot[...] = (
        jnp.where(row_token == lane, 1.0, 0.0).reshape(BLOCK * group, LANES).astype(hot.dtype)
    )

    def fill_bias(block, carry):
        base = me * rows
        token = base + block * BLOCK + lax.broadcasted_iota(jnp.int32, (1, LANES), 1)
        first = jnp.zeros((1, LANES), jnp.int32)
        end = jnp.int32(0)
        for d in range(lengths.shape[1]):
            end = end + lengths[0, d]
            first = jnp.where(token >= end, end, first)
        key = base + lax.broadcasted_iota(jnp.int32, (rows, LANES), 0)
        allowed = (key >= first) & (key <= token)
        bias_own[block] = jnp.where(allowed, 0.0, MASKED).astype(bias_own.dtype)
        key = base - 2 * rows + lax.broadcasted_iota(jnp.int32, (2 * rows, LANES), 0)
        bias_win[block] = jnp.where(key >= first, 0.0, MASKED).astype(bias_win.dtype)
        return carry

    lax.fori_loop(0, blocks - 1, fill_bias, 0)
    forward(0)

    @pl.when(hands)
    def _():
        spare_copy().wait_recv()
        hand_copy().start()

    lax.fori_loop(blocks - 1, blocks, fill_bias, 0)

    def queries_of(h, block):
        at = pl.ds(pl.multiple_of(block * BLOCK, BLOCK), BLOCK)
        q = qbuf[h, at].reshape(BLOCK * group, width)
        return jnp.concatenate([q, hot[...]], axis=1)

    def score_own(h, block, span, scores, tops):
        score_tile(
            queries_of(h, block), own[0, h, 0:span, :], bias_own[block, 0:span], None, scores, tops
        )

    def value_own(h, block, span, scores, tops):
        at = h * blocks + block
        state[at] = weigh(scores, tops, own[1, h, 0:span, :])
        state_top[at] = tops[...]

    def score_win(h, block, start, scores, tops):
        before = state_top[h * blocks + block]
        score_tile(
            queries_of(h, block), win[0, h, start:, :], bias_win[block, start:], before, scores, tops
        )

    def value_win(h, block, start, scores, tops):
        at = h * blocks + block
        total = weigh(scores, tops, win[1, h, start:, :])
        result = merged(total, state[at], state_top[at], tops[...])
        out[
            pl.ds(pl.multiple_of(block * BLOCK, BLOCK), BLOCK),
            pl.ds(pl.multiple_of(h * group, group), group),
            :,
        ] = result.reshape(BLOCK, group, width).astype(out.dtype)

    pairs = heads * half
    near_half, far_half = rows // 2, 0

    def pair_at(index, most):
        index = jnp.minimum(index, most - 1)
        return lax.div(index, half), lax.rem(index, half)

    for h in range(heads):
        q_copy(h).wait()

    score_own(0, 0, rows // 2, scores_a, tops_a)

    def own_lap(lap, carry):
        forward_some(jnp.maximum(lax.div(3 * lap, 2), 1), lax.div(3 * lap + 3, 2))

        for i in range(half):
            h, j = pair_at(lap * half + i, pairs)
            next_h, next_j = pair_at(lap * half + i + 1, pairs)
            score_own(h, j + half, rows, scores_b, tops_b)
            value_own(h, j, rows // 2, scores_a, tops_a)
            score_own(next_h, next_j, rows // 2, scores_a, tops_a)
            value_own(h, j + half, rows, scores_b, tops_b)
        return carry

    lax.fori_loop(0, heads, own_lap, 0)

    arrive(0, 0)
    score_win(0, 0, far_half, scores_a, tops_a)
    laps = half // STRIDE
    early = 3 * heads // 2
    last = heads - 1

    def win_lap(lap, carry):
        h, part = lax.div(lap, laps), lax.rem(lap, laps)

        first = early + lax.div(3 * lap, 2)
        forward_some(first, jnp.minimum(early + lax.div(3 * lap + 3, 2), chunks))

        @pl.when(part == 0)
        def _():
            arrive(h, 1)

        @pl.when((part == laps - 1) & (h + 1 < last))
        def _():
            arrive(h + 1, 0)

        for i in range(STRIDE):
            h, j = pair_at(lap * STRIDE + i, last * half)
            next_h, next_j = pair_at(lap * STRIDE + i + 1, last * half)
            score_win(h, j + half, near_half, scores_b, tops_b)
            value_win(h, j, far_half, scores_a, tops_a)
            score_win(next_h, next_j, far_half, scores_a, tops_a)
            value_win(h, j + half, near_half, scores_b, tops_b)
        return carry

    lax.fori_loop(0, last * laps, win_lap, 0)

    for c in range(early + 3 * last * laps // 2, chunks):
        forward(c)
    last_q[...] = qbuf[last]
    last_state[...] = state[last * blocks :]
    last_top[...] = state_top[last * blocks :]
    for part in range(2):
        arrive(last, part)
        last_win[part] = win[part, last]

    for c in range(chunks):

        @pl.when(has_up)
        def _():
            far_copy(c).wait_send()

        @pl.when(even | (has_down if c < chunks - 1 else False))
        def _():
            near_copy(c).wait_send()

    @pl.when(lends | hands)
    def _():
        spare_copy().wait_send()


def finish_kernel(lengths, done, win, qbuf, hot, bias_win, state, state_top, out_hbm, obuf, scores_a,
                  scores_b, tops_a, tops_b, done_sem, osem):
    rows, group, width = qbuf.shape
    blocks = rows // BLOCK
    half = blocks // 2
    laps = half // STRIDE
    ahead = done.shape[1]
    base = lax.axis_index("ctx") * rows

    ready = pltpu.make_async_copy(done, out_hbm.at[:, 0:ahead, :], done_sem)
    ready.start()

    def o_copy(block):
        at = pl.ds(pl.multiple_of(block * BLOCK, BLOCK), STRIDE * BLOCK)
        return pltpu.make_async_copy(
            obuf.at[at], out_hbm.at[at, ahead:, :], osem.at[lax.div(block, STRIDE)]
        )

    def first_of(token):
        first, end = jnp.int32(0), jnp.int32(0)
        for d in range(lengths.shape[1]):
            end = end + lengths[0, d]
            first = jnp.where(token >= end, end, first)
        return first

    def at_rows(block):
        return pl.ds(pl.multiple_of(block * BLOCK, BLOCK), BLOCK)

    def score(block, start, scores, tops):
        q = qbuf[at_rows(block)].reshape(BLOCK * group, width)
        q = jnp.concatenate([q, hot[...]], axis=1)
        keys, before = win[0, start:, :], state_top[block]
        score_tile(q, keys, bias_win[block, start:], before, scores, tops)

    def put(block, result):
        obuf[at_rows(block)] = result.reshape(BLOCK, group, width).astype(obuf.dtype)

    def value(block, start, scores, tops):
        total = weigh(scores, tops, win[1, start:, :])
        put(block, merged(total, state[block], state_top[block], tops[...]))

    def leave(lap):
        o_copy(lap * STRIDE).start()
        o_copy(lap * STRIDE + half).start()

    first = first_of(base)
    reach = first - (base - 2 * rows)
    busy = jnp.where(
        first >= base, 0, jnp.where(first_of(base + STRIDE * BLOCK) >= base, 1, laps)
    )

    for low, high, edge in ((-rows, rows // 2, 0), (rows // 2, rows, rows // 2), (rows, 2 * rows, rows)):

        @pl.when((reach >= low) & (reach < high))
        def _():
            far, near = edge, max(edge, rows // 2)
            score(0, far, scores_a, tops_a)

            def lap_of(lap, carry):
                for i in range(0, STRIDE, 2) if edge == 0 else ():
                    j = lap * STRIDE + i
                    score(j + 1, far, scores_b, tops_b)
                    value(j, far, scores_a, tops_a)
                    score(jnp.minimum(j + 2, half - 1), far, scores_a, tops_a)
                    value(j + 1, far, scores_b, tops_b)
                    for block in (j + half, j + half + 1):
                        put(block, normalized(state[block]))
                for i in range(STRIDE) if edge > 0 else ():
                    j = lap * STRIDE + i
                    later = jnp.minimum(j + 1, half - 1)
                    score(j + half, near, scores_b, tops_b)
                    value(j, far, scores_a, tops_a)
                    score(later, far, scores_a, tops_a)
                    value(j + half, near, scores_b, tops_b)
                leave(lap)
                return carry

            lax.fori_loop(0, busy, lap_of, 0)

    def rest(lap, carry):
        for i in range(STRIDE):
            for block in (lap * STRIDE + i, lap * STRIDE + i + half):
                put(block, normalized(state[block]))
        leave(lap)
        return carry

    lax.fori_loop(busy, laps, rest, 0)

    for lap in range(2 * laps):
        o_copy(lap * STRIDE).wait()
    ready.wait()


def body(count, queries, keys, values, doc_lengths):
    rows, query_heads, width = queries.shape
    heads = keys.shape[1]
    group = query_heads // heads
    blocks = rows // BLOCK
    chunks = 2 * PIECES * heads
    any_space = pl.BlockSpec(memory_space=pl.ANY)
    smem = pl.BlockSpec(memory_space=pltpu.SMEM)
    vmem = pl.BlockSpec(memory_space=pltpu.VMEM)
    work = [
        pltpu.VMEM((BLOCK * group, 2 * rows), jnp.float32),
        pltpu.VMEM((BLOCK * group, 2 * rows), jnp.float32),
        pltpu.VMEM((BLOCK * group, LANES), jnp.float32),
        pltpu.VMEM((BLOCK * group, LANES), jnp.float32),
    ]
    carried = pl.pallas_call(
        functools.partial(gather_kernel, count),
        out_shape=[
            pltpu.VMEM((rows, query_heads - group, width), queries.dtype),
            pltpu.VMEM((2, 2 * rows, width), keys.dtype),
            pltpu.VMEM((rows, group, width), queries.dtype),
            pltpu.VMEM((BLOCK * group, LANES), queries.dtype),
            pltpu.VMEM((blocks, 2 * rows, LANES), queries.dtype),
            pltpu.VMEM((blocks, BLOCK * group, 2 * width), jnp.float32),
            pltpu.VMEM((blocks, BLOCK * group, LANES), jnp.float32),
        ],
        in_specs=[smem, any_space, any_space, any_space],
        out_specs=[vmem] * 7,
        scratch_shapes=[
            pltpu.VMEM((2, heads, rows, width), keys.dtype),
            pltpu.VMEM((2, heads, 2 * rows, width), keys.dtype),
            pltpu.VMEM((heads, rows, group, width), queries.dtype),
            pltpu.VMEM((heads * blocks, BLOCK * group, 2 * width), jnp.float32),
            pltpu.VMEM((heads * blocks, BLOCK * group, LANES), jnp.float32),
            pltpu.VMEM((2, rows, heads, width), keys.dtype),
            pltpu.VMEM((rows * heads, width), jnp.float32),
            pltpu.VMEM((blocks, rows, LANES), queries.dtype),
            *work,
            pltpu.VMEM((rows // PIECES, width), keys.dtype),
            pltpu.SemaphoreType.DMA((heads,)),
            pltpu.SemaphoreType.DMA((2,)),
            pltpu.SemaphoreType.DMA((chunks,)),
            pltpu.SemaphoreType.DMA((chunks,)),
            pltpu.SemaphoreType.DMA((chunks,)),
            pltpu.SemaphoreType.DMA((chunks,)),
            pltpu.SemaphoreType.DMA((2,)),
        ],
        compiler_params=pltpu.CompilerParams(
            collective_id=0, has_side_effects=True, vmem_limit_bytes=44 * 1024 * 1024
        ),
    )(doc_lengths, queries, keys, values)
    return pl.pallas_call(
        finish_kernel,
        out_shape=jax.ShapeDtypeStruct(queries.shape, queries.dtype),
        in_specs=[smem] + [vmem] * 7,
        out_specs=any_space,
        scratch_shapes=[
            pltpu.VMEM((rows, group, width), queries.dtype),
            *work,
            pltpu.SemaphoreType.DMA,
            pltpu.SemaphoreType.DMA((blocks // STRIDE,)),
        ],
        compiler_params=pltpu.CompilerParams(vmem_limit_bytes=12 * 1024 * 1024),
    )(doc_lengths, *carried)


def solution(mesh):
    placed = (
        P(("dp", "ctx"), None, None),
        P(("dp", "ctx"), None, None),
        P(("dp", "ctx"), None, None),
        P("dp", None),
    )
    return jax.shard_map(
        functools.partial(body, mesh.shape["ctx"]),
        mesh=mesh,
        in_specs=placed,
        out_specs=P(("dp", "ctx"), None, None),
        check_vma=False,
    )
```

```python
import functools
import math

import jax
import jax.numpy as jnp
from jax import lax
from jax.experimental import pallas as pl
from jax.experimental.pallas import tpu as pltpu
from jax.sharding import PartitionSpec as P

LANES = 128
BLOCK = 64
PIECES = 2
STRIDE = 2
MASKED = -1e30
MESH = pl.DeviceIdType.MESH


def product(q, keys):
    return lax.dot_general(q, keys, (((1,), (1,)), ((), ())), preferred_element_type=jnp.float32)


def rate_of(width):
    return math.log2(math.e) / math.sqrt(width)


def weigh(scores, tops, values):
    span, width = values.shape
    ones = jnp.ones((span, LANES), values.dtype)
    top = jnp.concatenate([tops[...]] * (span // LANES), axis=1)
    weights = jnp.exp2((scores[:, 0:span] - top) * rate_of(width)).astype(values.dtype)
    return jnp.dot(
        weights, jnp.concatenate([values, ones], axis=1), preferred_element_type=jnp.float32
    )


def score_tile(q, keys, bias, before, scores, tops):
    found = product(q, jnp.concatenate([keys, bias], axis=1))
    scores[:, 0 : keys.shape[0]] = found
    best = jnp.broadcast_to(jnp.max(found, axis=1, keepdims=True), tops.shape)
    tops[...] = best if before is None else jnp.maximum(best, before)


def normalized(total):
    width = total.shape[1] // 2
    return total[:, :width] / total[:, width:]


def merged(total, state, state_top, tops):
    scale = jnp.exp2((state_top - tops) * rate_of(total.shape[1] // 2))
    return normalized(total + state * jnp.concatenate([scale, scale], axis=1))


def gather_kernel(count, lengths, q_hbm, k_hbm, v_hbm, out, last_win, last_q, hot, bias_win,
                  last_state, last_top, own, win, qbuf, state, state_top, raw, flat, bias_own,
                  scores_a, scores_b, tops_a, tops_b, spare, qsem, rawsem, far_send,
                  far_recv, near_send, near_recv, spare_sem):
    rows, heads, width = k_hbm.shape
    group = q_hbm.shape[1] // heads
    blocks = rows // BLOCK
    half = blocks // 2
    piece_rows = rows // PIECES
    spare_rows = piece_rows // 2
    per_head = 2 * PIECES
    chunks = per_head * heads
    me = lax.axis_index("ctx")
    odd = lax.rem(me, 2) == 1
    even = jnp.logical_not(odd)
    partner = jnp.where(odd, me - 1, me + 1)
    has_up = me + 2 < count
    has_down = me >= 2
    lends = odd & (me + 1 < count)
    hands = even & has_up

    barrier = pltpu.get_barrier_semaphore()

    def greet(other):
        pl.semaphore_signal(barrier, inc=1, device_id={"ctx": other}, device_id_type=MESH)

    def q_copy(h):
        return pltpu.make_async_copy(
            q_hbm.at[:, pl.ds(h * group, group), :], qbuf.at[h], qsem.at[h]
        )

    def raw_copy(part):
        return pltpu.make_async_copy((k_hbm, v_hbm)[part], raw.at[part], rawsem.at[part])

    def place(c):
        h, rest = lax.div(c, per_head), lax.rem(c, per_head)
        part, piece = lax.div(rest, PIECES), lax.rem(rest, PIECES)
        return part, h, pl.multiple_of(piece * piece_rows, piece_rows)

    def far_copy(c):
        part, h, first = place(c)
        return pltpu.make_async_remote_copy(
            src_ref=own.at[part, h, pl.ds(first, piece_rows), :],
            dst_ref=win.at[part, h, pl.ds(first, piece_rows), :],
            send_sem=far_send.at[c],
            recv_sem=far_recv.at[c],
            device_id={"ctx": me + 2},
            device_id_type=MESH,
        )

    def near_copy(c):
        part, h, first = place(c)
        return pltpu.make_async_remote_copy(
            src_ref=own.at[part, h, pl.ds(first, piece_rows), :],
            dst_ref=win.at[part, h, pl.ds(rows + first, piece_rows), :],
            send_sem=near_send.at[c],
            recv_sem=near_recv.at[c],
            device_id={"ctx": partner},
            device_id_type=MESH,
        )

    def relay_copy(c):
        part, h, first = place(c)
        return pltpu.make_async_remote_copy(
            src_ref=win.at[part, h, pl.ds(first, piece_rows), :],
            dst_ref=win.at[part, h, pl.ds(rows + first, piece_rows), :],
            send_sem=near_send.at[c],
            recv_sem=near_recv.at[c],
            device_id={"ctx": partner},
            device_id_type=MESH,
        )

    def spare_copy():
        part, h, first = place(chunks - 1)
        return pltpu.make_async_remote_copy(
            src_ref=own.at[part, h, pl.ds(first, spare_rows), :],
            dst_ref=spare,
            send_sem=spare_sem.at[0],
            recv_sem=spare_sem.at[1],
            device_id={"ctx": partner},
            device_id_type=MESH,
        )

    def hand_copy():
        part, h, first = place(chunks - 1)
        return pltpu.make_async_remote_copy(
            src_ref=spare,
            dst_ref=win.at[part, h, pl.ds(rows + first, spare_rows), :],
            send_sem=spare_sem.at[0],
            recv_sem=near_recv.at[chunks - 1],
            device_id={"ctx": me + 2},
            device_id_type=MESH,
        )

    def rest_copy():
        part, h, first = place(chunks - 1)
        first = first + spare_rows
        return pltpu.make_async_remote_copy(
            src_ref=win.at[part, h, pl.ds(first, piece_rows - spare_rows), :],
            dst_ref=win.at[part, h, pl.ds(rows + first, piece_rows - spare_rows), :],
            send_sem=near_send.at[chunks - 1],
            recv_sem=near_recv.at[chunks - 1],
            device_id={"ctx": partner},
            device_id_type=MESH,
        )

    def launch(c):
        @pl.when(has_up)
        def _():
            far_copy(c).start()

        @pl.when(even)
        def _():
            near_copy(c).start()

    def forward(c):
        @pl.when(odd & has_down)
        def _():
            far_copy(c).wait_recv()

            @pl.when(c < chunks - 1)
            def _():
                relay_copy(c).start()

            @pl.when(c == chunks - 1)
            def _():
                rest_copy().start()

    def forward_some(first, limit):
        for c in (first, first + 1):

            @pl.when(c < limit)
            def _():
                forward(c)

    def arrive(h, part):
        for piece in range(PIECES):
            c = h * per_head + part * PIECES + piece

            @pl.when(even & has_down)
            def _():
                far_copy(c).wait_recv()

            @pl.when(me >= 1)
            def _():
                near_copy(c).wait_recv()

    greet(partner)

    @pl.when(has_up)
    def _():
        greet(me + 2)

    @pl.when(has_down)
    def _():
        greet(me - 2)

    for part in range(2):
        raw_copy(part).start()
    for part in range(2):
        raw_copy(part).wait()
        flat[...] = raw[part].astype(jnp.float32).reshape(rows * heads, width)
        for h in range(heads):
            own[part, h] = flat[pl.ds(h, rows, stride=heads), :].astype(own.dtype)
        if part == 0:
            pl.semaphore_wait(
                barrier, 1 + has_up.astype(jnp.int32) + has_down.astype(jnp.int32)
            )
            for c in range(PIECES):
                launch(c)

    @pl.when(lends)
    def _():
        spare_copy().start()

    def launch_rest(c, carry):
        launch(c)
        return carry

    lax.fori_loop(PIECES, chunks, launch_rest, 0)

    for h in range(heads):
        q_copy(h).start()

    @pl.when(me < 2)
    def _():
        win[:, :, 0:rows, :] = jnp.zeros((2, heads, rows, width), win.dtype)

    @pl.when(me < 1)
    def _():
        win[:, :, rows : 2 * rows, :] = jnp.zeros((2, heads, rows, width), win.dtype)

    row_token = lax.broadcasted_iota(jnp.int32, (BLOCK, group, LANES), 0)
    lane = lax.broadcasted_iota(jnp.int32, (BLOCK, group, LANES), 2)
    hot[...] = (
        jnp.where(row_token == lane, 1.0, 0.0).reshape(BLOCK * group, LANES).astype(hot.dtype)
    )

    def fill_bias(block, carry):
        base = me * rows
        token = base + block * BLOCK + lax.broadcasted_iota(jnp.int32, (1, LANES), 1)
        first = jnp.zeros((1, LANES), jnp.int32)
        end = jnp.int32(0)
        for d in range(lengths.shape[1]):
            end = end + lengths[0, d]
            first = jnp.where(token >= end, end, first)
        key = base + lax.broadcasted_iota(jnp.int32, (rows, LANES), 0)
        allowed = (key >= first) & (key <= token)
        bias_own[block] = jnp.where(allowed, 0.0, MASKED).astype(bias_own.dtype)
        key = base - 2 * rows + lax.broadcasted_iota(jnp.int32, (2 * rows, LANES), 0)
        bias_win[block] = jnp.where(key >= first, 0.0, MASKED).astype(bias_win.dtype)
        return carry

    lax.fori_loop(0, blocks - 1, fill_bias, 0)
    forward(0)

    @pl.when(hands)
    def _():
        spare_copy().wait_recv()
        hand_copy().start()

    lax.fori_loop(blocks - 1, blocks, fill_bias, 0)

    def queries_of(h, block):
        at = pl.ds(pl.multiple_of(block * BLOCK, BLOCK), BLOCK)
        q = qbuf[h, at].reshape(BLOCK * group, width)
        return jnp.concatenate([q, hot[...]], axis=1)

    def score_own(h, block, span, scores, tops):
        score_tile(
            queries_of(h, block), own[0, h, 0:span, :], bias_own[block, 0:span], None, scores, tops
        )

    def value_own(h, block, span, scores, tops):
        at = h * blocks + block
        state[at] = weigh(scores, tops, own[1, h, 0:span, :])
        state_top[at] = tops[...]

    def score_win(h, block, start, scores, tops):
        before = state_top[h * blocks + block]
        score_tile(
            queries_of(h, block), win[0, h, start:, :], bias_win[block, start:], before, scores, tops
        )

    def value_win(h, block, start, scores, tops):
        at = h * blocks + block
        total = weigh(scores, tops, win[1, h, start:, :])
        result = merged(total, state[at], state_top[at], tops[...])
        out[
            pl.ds(pl.multiple_of(block * BLOCK, BLOCK), BLOCK),
            pl.ds(pl.multiple_of(h * group, group), group),
            :,
        ] = result.reshape(BLOCK, group, width).astype(out.dtype)

    pairs = heads * half
    near_half, far_half = rows // 2, 0

    def pair_at(index, most):
        index = jnp.minimum(index, most - 1)
        return lax.div(index, half), lax.rem(index, half)

    for h in range(heads):
        q_copy(h).wait()

    score_own(0, 0, rows // 2, scores_a, tops_a)

    def own_lap(lap, carry):
        forward_some(jnp.maximum(lax.div(3 * lap, 2), 1), lax.div(3 * lap + 3, 2))

        for i in range(half):
            h, j = pair_at(lap * half + i, pairs)
            next_h, next_j = pair_at(lap * half + i + 1, pairs)
            score_own(h, j + half, rows, scores_b, tops_b)
            value_own(h, j, rows // 2, scores_a, tops_a)
            score_own(next_h, next_j, rows // 2, scores_a, tops_a)
            value_own(h, j + half, rows, scores_b, tops_b)
        return carry

    lax.fori_loop(0, heads, own_lap, 0)

    arrive(0, 0)
    score_win(0, 0, far_half, scores_a, tops_a)
    laps = half // STRIDE
    early = 3 * heads // 2
    last = heads - 1

    def win_lap(lap, carry):
        h, part = lax.div(lap, laps), lax.rem(lap, laps)

        first = early + lax.div(3 * lap, 2)
        forward_some(first, jnp.minimum(early + lax.div(3 * lap + 3, 2), chunks))

        @pl.when(part == 0)
        def _():
            arrive(h, 1)

        @pl.when((part == laps - 1) & (h + 1 < last))
        def _():
            arrive(h + 1, 0)

        for i in range(STRIDE):
            h, j = pair_at(lap * STRIDE + i, last * half)
            next_h, next_j = pair_at(lap * STRIDE + i + 1, last * half)
            score_win(h, j + half, near_half, scores_b, tops_b)
            value_win(h, j, far_half, scores_a, tops_a)
            score_win(next_h, next_j, far_half, scores_a, tops_a)
            value_win(h, j + half, near_half, scores_b, tops_b)
        return carry

    lax.fori_loop(0, last * laps, win_lap, 0)

    for c in range(early + 3 * last * laps // 2, chunks):
        forward(c)
    last_q[...] = qbuf[last]
    last_state[...] = state[last * blocks :]
    last_top[...] = state_top[last * blocks :]
    for part in range(2):
        arrive(last, part)
        last_win[part] = win[part, last]

    for c in range(chunks):

        @pl.when(has_up)
        def _():
            far_copy(c).wait_send()

        @pl.when(even | (has_down if c < chunks - 1 else False))
        def _():
            near_copy(c).wait_send()

    @pl.when(lends | hands)
    def _():
        spare_copy().wait_send()

    @pl.when(odd & has_down)
    def _():
        rest_copy().wait_send()


def finish_kernel(lengths, done, win, qbuf, hot, bias_win, state, state_top, out_hbm, obuf, scores_a,
                  scores_b, tops_a, tops_b, done_sem, osem):
    rows, group, width = qbuf.shape
    blocks = rows // BLOCK
    half = blocks // 2
    laps = half // STRIDE
    ahead = done.shape[1]
    base = lax.axis_index("ctx") * rows

    ready = pltpu.make_async_copy(done, out_hbm.at[:, 0:ahead, :], done_sem)
    ready.start()

    def o_copy(block):
        at = pl.ds(pl.multiple_of(block * BLOCK, BLOCK), STRIDE * BLOCK)
        return pltpu.make_async_copy(
            obuf.at[at], out_hbm.at[at, ahead:, :], osem.at[lax.div(block, STRIDE)]
        )

    def first_of(token):
        first, end = jnp.int32(0), jnp.int32(0)
        for d in range(lengths.shape[1]):
            end = end + lengths[0, d]
            first = jnp.where(token >= end, end, first)
        return first

    def at_rows(block):
        return pl.ds(pl.multiple_of(block * BLOCK, BLOCK), BLOCK)

    def score(block, start, scores, tops):
        q = qbuf[at_rows(block)].reshape(BLOCK * group, width)
        q = jnp.concatenate([q, hot[...]], axis=1)
        keys, before = win[0, start:, :], state_top[block]
        score_tile(q, keys, bias_win[block, start:], before, scores, tops)

    def put(block, result):
        obuf[at_rows(block)] = result.reshape(BLOCK, group, width).astype(obuf.dtype)

    def value(block, start, scores, tops):
        total = weigh(scores, tops, win[1, start:, :])
        put(block, merged(total, state[block], state_top[block], tops[...]))

    def leave(lap):
        o_copy(lap * STRIDE).start()
        o_copy(lap * STRIDE + half).start()

    first = first_of(base)
    reach = first - (base - 2 * rows)
    busy = jnp.where(
        first >= base, 0, jnp.where(first_of(base + STRIDE * BLOCK) >= base, 1, laps)
    )

    for low, high, edge in ((-rows, rows // 2, 0), (rows // 2, rows, rows // 2), (rows, 2 * rows, rows)):

        @pl.when((reach >= low) & (reach < high))
        def _():
            far, near = edge, max(edge, rows // 2)
            score(0, far, scores_a, tops_a)

            def lap_of(lap, carry):
                for i in range(0, STRIDE, 2) if edge == 0 else ():
                    j = lap * STRIDE + i
                    score(j + 1, far, scores_b, tops_b)
                    value(j, far, scores_a, tops_a)
                    score(jnp.minimum(j + 2, half - 1), far, scores_a, tops_a)
                    value(j + 1, far, scores_b, tops_b)
                    for block in (j + half, j + half + 1):
                        put(block, normalized(state[block]))
                for i in range(STRIDE) if edge > 0 else ():
                    j = lap * STRIDE + i
                    later = jnp.minimum(j + 1, half - 1)
                    score(j + half, near, scores_b, tops_b)
                    value(j, far, scores_a, tops_a)
                    score(later, far, scores_a, tops_a)
                    value(j + half, near, scores_b, tops_b)
                leave(lap)
                return carry

            lax.fori_loop(0, busy, lap_of, 0)

    def rest(lap, carry):
        for i in range(STRIDE):
            for block in (lap * STRIDE + i, lap * STRIDE + i + half):
                put(block, normalized(state[block]))
        leave(lap)
        return carry

    lax.fori_loop(busy, laps, rest, 0)

    for lap in range(2 * laps):
        o_copy(lap * STRIDE).wait()
    ready.wait()


def body(count, queries, keys, values, doc_lengths):
    rows, query_heads, width = queries.shape
    heads = keys.shape[1]
    group = query_heads // heads
    blocks = rows // BLOCK
    chunks = 2 * PIECES * heads
    any_space = pl.BlockSpec(memory_space=pl.ANY)
    smem = pl.BlockSpec(memory_space=pltpu.SMEM)
    vmem = pl.BlockSpec(memory_space=pltpu.VMEM)
    work = [
        pltpu.VMEM((BLOCK * group, 2 * rows), jnp.float32),
        pltpu.VMEM((BLOCK * group, 2 * rows), jnp.float32),
        pltpu.VMEM((BLOCK * group, LANES), jnp.float32),
        pltpu.VMEM((BLOCK * group, LANES), jnp.float32),
    ]
    carried = pl.pallas_call(
        functools.partial(gather_kernel, count),
        out_shape=[
            pltpu.VMEM((rows, query_heads - group, width), queries.dtype),
            pltpu.VMEM((2, 2 * rows, width), keys.dtype),
            pltpu.VMEM((rows, group, width), queries.dtype),
            pltpu.VMEM((BLOCK * group, LANES), queries.dtype),
            pltpu.VMEM((blocks, 2 * rows, LANES), queries.dtype),
            pltpu.VMEM((blocks, BLOCK * group, 2 * width), jnp.float32),
            pltpu.VMEM((blocks, BLOCK * group, LANES), jnp.float32),
        ],
        in_specs=[smem, any_space, any_space, any_space],
        out_specs=[vmem] * 7,
        scratch_shapes=[
            pltpu.VMEM((2, heads, rows, width), keys.dtype),
            pltpu.VMEM((2, heads, 2 * rows, width), keys.dtype),
            pltpu.VMEM((heads, rows, group, width), queries.dtype),
            pltpu.VMEM((heads * blocks, BLOCK * group, 2 * width), jnp.float32),
            pltpu.VMEM((heads * blocks, BLOCK * group, LANES), jnp.float32),
            pltpu.VMEM((2, rows, heads, width), keys.dtype),
            pltpu.VMEM((rows * heads, width), jnp.float32),
            pltpu.VMEM((blocks, rows, LANES), queries.dtype),
            *work,
            pltpu.VMEM((rows // PIECES // 2, width), keys.dtype),
            pltpu.SemaphoreType.DMA((heads,)),
            pltpu.SemaphoreType.DMA((2,)),
            pltpu.SemaphoreType.DMA((chunks,)),
            pltpu.SemaphoreType.DMA((chunks,)),
            pltpu.SemaphoreType.DMA((chunks,)),
            pltpu.SemaphoreType.DMA((chunks,)),
            pltpu.SemaphoreType.DMA((2,)),
        ],
        compiler_params=pltpu.CompilerParams(
            collective_id=0, has_side_effects=True, vmem_limit_bytes=44 * 1024 * 1024
        ),
    )(doc_lengths, queries, keys, values)
    return pl.pallas_call(
        finish_kernel,
        out_shape=jax.ShapeDtypeStruct(queries.shape, queries.dtype),
        in_specs=[smem] + [vmem] * 7,
        out_specs=any_space,
        scratch_shapes=[
            pltpu.VMEM((rows, group, width), queries.dtype),
            *work,
            pltpu.SemaphoreType.DMA,
            pltpu.SemaphoreType.DMA((blocks // STRIDE,)),
        ],
        compiler_params=pltpu.CompilerParams(vmem_limit_bytes=12 * 1024 * 1024),
    )(doc_lengths, *carried)


def solution(mesh):
    placed = (
        P(("dp", "ctx"), None, None),
        P(("dp", "ctx"), None, None),
        P(("dp", "ctx"), None, None),
        P("dp", None),
    )
    return jax.shard_map(
        functools.partial(body, mesh.shape["ctx"]),
        mesh=mesh,
        in_specs=placed,
        out_specs=P(("dp", "ctx"), None, None),
        check_vma=False,
    )
```
